32 devices in a mesh: blk: 2 (over x), rows: 16 (over z, y, core).
Axes of the slice: x: 2, y: 2, z: 4, core: 2. Of those that a mesh axis runs over, the one named last changes fastest.
Arguments:
- features: bfloat16 [8192, 128], P(('blk', 'rows')), may hold values from -6 to 6
- labels: int32 [8192], P(('blk', 'rows')), may hold values from 0 to 6
- destination: int32 [8192, 1], P(('blk', 'rows')), may hold values from 0 to 15; in each aligned block of 256 rows (0 to 255, 256 to 511, ...) at most 32 rows name the same one
- centres: bfloat16 [8192, 128], P('blk'), may hold values from -6 to 6
- tri_inverse: float32 [8192, 8192], P('blk', 'rows'), may hold values from -1 to 2, as said below
- aux_inverse: float32 [8192, 8192], P('blk', 'rows'), may hold values from -1 to 2, as said below
Outputs:
- predictions: float32 [7, 16384], P(None, ('blk', 'rows'))
The draws below stay inside these ranges and needn't reach their ends.
Inputs may be any that keep to these rules, and one draw needn't show every extreme that they name: `destination`: in each aligned block of 256 rows (the rows of one device) no value occurs more than 32 times, and some value occurs exactly 32 times. `tri_inverse`: zero below the diagonal, positive on it. `aux_inverse`: zero below the diagonal, positive on it.
All inputs are finite; a program needn't handle non-finite values.
Results may differ from the reference program's by a relative error of at most 0.0003.
Values may be sent and summed in bfloat16 or wider, within the bound.
A program may use at most 128 MiB of HBM per device.

```python
import math
import jax
import jax.numpy as jnp
import numpy as np
from jax import lax

D = 128
M = 8192
CLASSES = 7
ITERS = 2
ROWS_DEV = 256
CAP = 32
ROWS_ALL = 8192
SLOTS_ALL = 16384
N_BLK = 2
N_ROWS = 16


def triangle_draw(key):
    first_key, second_key = jax.random.split(key)
    row_ids = jnp.arange(M, dtype=jnp.int32)[:, None]
    col_ids = jnp.arange(M, dtype=jnp.int32)[None, :]
    spread = 0.6 / math.sqrt(M)
    upper = jax.random.normal(first_key, (M, M), jnp.float32) * spread
    diagonal = jax.random.uniform(second_key, (M,), jnp.float32, 0.7, 1.3)
    upper = jnp.clip(upper, -0.9, 0.9)
    return jnp.where(col_ids > row_ids, upper, 0.0) + jnp.where(col_ids == row_ids, diagonal[:, None], 0.0)


def draw_tri_inverse(key, part):
    return triangle_draw(jax.random.fold_in(key, 11))


def draw_aux_inverse(key, part):
    return triangle_draw(jax.random.fold_in(key, 23))


def place_ends(entries, stream_key, least, largest):
    index_at = [jax.random.randint(jax.random.fold_in(stream_key, axis), (), 0, length) for axis, length in enumerate(entries.shape)]
    widest = entries.shape.index(max(entries.shape))
    beside = index_at[:widest] + [(index_at[widest] + 1) % entries.shape[widest]] + index_at[widest + 1:]
    return entries.at[tuple(index_at)].set(least).at[tuple(beside)].set(largest)


def shard_levels(stream_key, dims, cuts, smallest, top_value):
    loudness, own = 1.0, jax.random.fold_in(stream_key, 6)
    for dim, blocks in cuts:
        steps = jnp.exp(jax.random.uniform(jax.random.fold_in(own, dim), (blocks,), jnp.float32, smallest / len(cuts), top_value / len(cuts)))
        loudness = loudness * jnp.repeat(steps, dims[dim] // blocks).reshape([-1 if axis == dim else 1 for axis in range(len(dims))])
    return loudness


def shared_out(stream_key, own, number, rows, number_of, top, limit, lean):
    sequence = jax.random.permutation(stream_key, number_of)
    packed, usual = load_shares(number_of, rows * top, limit, lean, True), load_shares(number_of, rows * top, limit, lean, False)
    places = jnp.arange(number_of)

    def named(tallies, offset_by):
        used = int((tallies > 0).sum())
        fixed = max(1, used // 4)
        moved = fixed + (places - fixed + offset_by * (used - fixed)) % max(1, number_of - fixed)
        return jnp.zeros((number_of,), jnp.int32).at[sequence[jnp.where(places < fixed, places, moved)]].set(jnp.asarray(tallies, jnp.int32))

    tallies = jnp.where(number % 4 == 0, named(packed, number // 4), named(usual, number - number // 4 - 1))
    mixed = jax.random.permutation(jax.random.fold_in(own, 3), number_of)
    donor, sink = mixed[0:number_of // 2 * 2:2], mixed[1:number_of // 2 * 2:2]
    room = jnp.minimum(tallies[donor] - 1, limit - tallies[sink]) // 2
    room = jnp.where((donor == sequence[0]) | (sink == sequence[0]) | (tallies[sink] == 0), 0, jnp.maximum(room, 0))
    moved = jax.random.randint(jax.random.fold_in(own, 4), (number_of // 2,), 0, 1 << 20) % (room + 1)
    tallies = tallies.at[donor].add(-moved).at[sink].add(moved)
    items = jnp.searchsorted(jnp.cumsum(tallies), jnp.arange(rows * top), side="right").astype(jnp.int32)
    listing = items.reshape(top, rows).T
    listing = listing[jax.random.permutation(jax.random.fold_in(own, 1), rows)]
    offset_by = jax.random.randint(jax.random.fold_in(own, 2), (rows, 1), 0, top)
    return jnp.take_along_axis(listing, (jnp.arange(top)[None, :] + offset_by) % top, axis=1)


def load_shares(amount, total, bound, skew, full):
    portions = [(1 << 20) // math.isqrt(rank ** skew) + 1 for rank in range(1, amount + 1)]
    largest = bound if full else min(bound, max(-(-total // amount), total * portions[0] // sum(portions)))
    least = 1 if total - largest >= amount - 1 else 0
    holding, surplus = [largest] + [least] * (amount - 1), total - largest - least * (amount - 1)
    while surplus > 0:
        movable = [i for i in range(1, amount) if holding[i] < largest] or [i for i in range(1, amount) if holding[i] < bound]
        mass, remaining = sum([portions[i] for i in movable]), surplus
        for i in movable:
            addition = min(bound - holding[i], max(1, remaining * portions[i] // mass), surplus)
            holding[i] = holding[i] + addition
            surplus = surplus - addition
    return np.array(holding)


def centred(own_key, shape, width, limit, shards=(), kind=jnp.bfloat16):
    entries = jax.random.normal(own_key, shape, jnp.float32) * width
    if len(shards) > 0:
        entries = shard_levels(own_key, shape, shards, -0.22, 0.18) * entries
    return jnp.clip(entries, min=-limit, max=limit).astype(kind)


def setup_inputs(seed: int = 0) -> dict:
    seeds = jax.random.split(jax.random.key(seed), 7)
    features = centred(seeds[0], (ROWS_ALL, D), 1.0, 6.0, ((0, 32),))
    labels = place_ends(jax.random.randint(seeds[1], (ROWS_ALL,), 0, CLASSES), jax.random.fold_in(seeds[1], 1), 0, CLASSES - 1).astype(jnp.int32)
    destination_keys = jax.random.split(jax.random.fold_in(seeds[2], 1), ROWS_ALL // ROWS_DEV)
    destination_turns = jax.random.permutation(jax.random.fold_in(seeds[2], 3), ROWS_ALL // ROWS_DEV)
    destination = jax.vmap(lambda own, number: shared_out(jax.random.fold_in(seeds[2], 2), own, number, ROWS_DEV, N_ROWS, 1, CAP, 2))(destination_keys, destination_turns).reshape((ROWS_ALL, 1))
    centres = centred(seeds[3], (M, D), 1.0, 6.0, ((0, 2),))
    tri_inverse = draw_tri_inverse(jax.random.fold_in(seeds[6], 71), 0)
    aux_inverse = draw_aux_inverse(jax.random.fold_in(seeds[6], 71), 0)
    return dict(features=features, labels=labels, destination=destination, centres=centres, tri_inverse=tri_inverse, aux_inverse=aux_inverse)


ridge_weight = 0.1
highest = lax.Precision.HIGHEST


def as_bf16(values):
    return lax.optimization_barrier(values.astype(jnp.bfloat16)).astype(jnp.float32)


def reference(features, labels, destination, centres, tri_inverse, aux_inverse):
    scale = 2.0 / D
    count_all = float(ROWS_ALL)
    centre_f = centres.astype(jnp.float32)
    centre_norm = jnp.sum(centre_f * centre_f, axis=1)
    block = math.gcd(ROWS_ALL, 1024)
    stacked = features.reshape(ROWS_ALL // block, block, D)
    class_ids = jnp.arange(CLASSES, dtype=jnp.int32)[:, None]
    targets = jnp.where(labels[None, :] == class_ids, 1.0, -1.0).astype(jnp.float32)
    stacked_targets = targets.reshape(CLASSES, ROWS_ALL // block, block).transpose(1, 0, 2)

    def tile_of(rows_x):
        rows_f = rows_x.astype(jnp.float32)
        rows_norm = jnp.sum(rows_f * rows_f, axis=1)
        inner = jnp.dot(rows_f, centre_f.T, precision=highest)
        return as_bf16(jnp.exp(-(rows_norm[:, None] + centre_norm[None, :] - 2.0 * inner) * scale))

    def gram(vector):
        low = as_bf16(vector)

        def visit(carry, rows_x):
            tile = tile_of(rows_x)
            image = as_bf16(jnp.dot(low, tile.T, precision=highest))
            return carry + jnp.dot(image, tile, precision=highest), None

        total, _ = lax.scan(visit, jnp.zeros((CLASSES, M), jnp.float32), stacked)
        return total / count_all

    def visit_targets(carry, pieces):
        rows_x, rows_targets = pieces
        return carry + jnp.dot(rows_targets, tile_of(rows_x), precision=highest), None

    kernel_targets, _ = lax.scan(visit_targets, jnp.zeros((CLASSES, M), jnp.float32), (stacked, stacked_targets))

    def forward(factor, vector):
        return jnp.dot(vector, factor.T, precision=highest)

    def backward(factor, vector):
        return jnp.dot(vector, factor, precision=highest)

    def system(vector):
        first = forward(aux_inverse, vector)
        second = forward(tri_inverse, first)
        third = backward(tri_inverse, gram(second))
        return backward(aux_inverse, third + ridge_weight * first)

    rhs = backward(aux_inverse, backward(tri_inverse, kernel_targets / count_all))
    solution = jnp.zeros((CLASSES, M), jnp.float32)
    residual = rhs
    direction = rhs
    norm_now = jnp.sum(residual * residual, axis=1, keepdims=True)
    for step in range(ITERS):
        image = system(direction)
        step_size = norm_now / jnp.sum(direction * image, axis=1, keepdims=True)
        solution = solution + step_size * direction
        residual = residual - step_size * image
        norm_next = jnp.sum(residual * residual, axis=1, keepdims=True)
        direction = residual + (norm_next / norm_now) * direction
        norm_now = norm_next
    coefficients = forward(tri_inverse, forward(aux_inverse, solution))
    low_coeff = as_bf16(coefficients)

    def score_block(rows_x):
        return jnp.dot(low_coeff, tile_of(rows_x).T, precision=highest)

    scores = lax.map(score_block, stacked).transpose(1, 0, 2).reshape(CLASSES, ROWS_ALL)

    devices = N_BLK * N_ROWS
    target = destination[:, 0].reshape(devices, ROWS_DEV)
    picks = (target[:, :, None] == jnp.arange(N_ROWS, dtype=jnp.int32)[None, None, :]).astype(jnp.int32)
    before = jnp.sum((jnp.cumsum(picks, axis=1) - picks) * picks, axis=2)
    device_id = jnp.arange(devices, dtype=jnp.int32)[:, None]
    group_of = device_id // N_ROWS
    source = device_id % N_ROWS
    slot = (((group_of * N_ROWS + target) * N_ROWS + source) * CAP + before).reshape(ROWS_ALL).astype(jnp.int32)
    predictions = jnp.zeros((CLASSES, SLOTS_ALL), jnp.float32).at[:, slot].set(scores)
    return predictions
```

```python
import functools

import jax
import jax.numpy as jnp
from jax import lax
from jax.experimental import pallas as pl
from jax.experimental.pallas import tpu as pltpu
from jax.sharding import PartitionSpec as P

CLASSES = 7
PAD = 8
MESH = pl.DeviceIdType.MESH
ridge_weight = 0.1
highest = lax.Precision.HIGHEST


def greet(peers, count):
    barrier = pltpu.get_barrier_semaphore()

    def hello(k, carry):
        pl.semaphore_signal(barrier, inc=1, device_id=peers(k), device_id_type=MESH)
        return carry

    lax.fori_loop(1, count, hello, 0)
    pl.semaphore_wait(barrier, count - 1)


def exchange(make, count, then):
    def send(k, carry):
        make(k).start()
        return carry

    def arrive(k, carry):
        make(k).wait_recv()
        return carry

    def left(k, carry):
        make(k).wait_send()
        return carry

    lax.fori_loop(1, count, send, 0)
    lax.fori_loop(1, count, arrive, 0)
    if then is not None:
        then()
    lax.fori_loop(1, count, left, 0)


def sum_kernel(kind, nb, nr, x_ref, o_ref, land, full, s1, r1, s2, r2):
    b, r = lax.axis_index("blk"), lax.axis_index("rows")
    n = nb * nr
    me = b * nr + r
    chunk = land.shape[2]

    def everyone(k):
        peer = lax.rem(me + k, n)
        return (peer // nr, lax.rem(peer, nr))

    greet(everyone, n)
    if kind == "all":
        parts, own, place = n, me, me
    elif kind == "rows":
        parts, own, place = nr, r, me
    else:
        parts, own, place = nb, b, r * nb + b

    def spot(index):
        return pl.ds(pl.multiple_of(index * chunk, chunk), chunk)

    def scatter(k):
        other = lax.rem(own + k, parts)
        if kind == "all":
            device = everyone(k)
        elif kind == "rows":
            device = (b, other)
        else:
            device = (other, r)
        return pltpu.make_async_remote_copy(
            src_ref=x_ref.at[:, spot(other)],
            dst_ref=land.at[own],
            send_sem=s1.at[k],
            recv_sem=r1.at[k],
            device_id=device,
            device_id_type=MESH,
        )

    def add_up():
        total = land[0]
        for index in range(1, parts):
            total = total + land[index]
        full[:, spot(place)] = total

    land[own] = x_ref[:, spot(own)]
    exchange(scatter, parts, add_up)

    def gather(k):
        return pltpu.make_async_remote_copy(
            src_ref=full.at[:, spot(place)],
            dst_ref=full.at[:, spot(place)],
            send_sem=s2.at[k],
            recv_sem=r2.at[k],
            device_id=everyone(k),
            device_id_type=MESH,
        )

    exchange(gather, n, None)
    o_ref[...] = full[...]


def swap_kernel(kind, nb, nr, x_ref, o_ref, land, s1, r1):
    b, r = lax.axis_index("blk"), lax.axis_index("rows")
    n = nb * nr
    me = b * nr + r
    if kind == "pair":
        parts, own = nb, b
    elif kind == "total":
        parts, own = n, me
    else:
        parts, own = nr, r

    def device(k):
        other = lax.rem(own + k, parts)
        if kind == "pair":
            return (other, r)
        if kind == "total":
            return (other // nr, lax.rem(other, nr))
        return (b, other)

    greet(device, parts)

    def make(k):
        source = x_ref.at[lax.rem(own + k, parts)] if kind == "move" else x_ref
        return pltpu.make_async_remote_copy(
            src_ref=source,
            dst_ref=land.at[own],
            send_sem=s1.at[k],
            recv_sem=r1.at[k],
            device_id=device(k),
            device_id_type=MESH,
        )

    land[own] = x_ref[own] if kind == "move" else x_ref[...]

    def finish():
        if kind == "move":
            o_ref[...] = land[...]
        else:
            total = land[0]
            for index in range(1, parts):
                total = total + land[index]
            o_ref[...] = total

    exchange(make, parts, finish)


def centre_kernel(nb, nr, x_ref, o_ref, local_sem, s1, r1):
    b, r = lax.axis_index("blk"), lax.axis_index("rows")
    rows = x_ref.shape[0]
    half = rows // 2
    core = lax.rem(r, 2)
    side, twin = (1 - b, r), (b, r + 1 - 2 * core)
    barrier = pltpu.get_barrier_semaphore()
    for peer in (side, twin):
        pl.semaphore_signal(barrier, inc=1, device_id=peer, device_id_type=MESH)
    pl.semaphore_wait(barrier, 2)
    mine = pltpu.make_async_copy(x_ref, o_ref.at[pl.ds(b * rows, rows)], local_sem)
    across = pltpu.make_async_remote_copy(
        src_ref=x_ref.at[pl.ds(core * half, half)],
        dst_ref=o_ref.at[pl.ds(b * rows + core * half, half)],
        send_sem=s1.at[0],
        recv_sem=r1.at[0],
        device_id=side,
        device_id_type=MESH,
    )
    across.start()
    mine.start()
    across.wait_recv()
    got = pl.ds((1 - b) * rows + core * half, half)
    beside = pltpu.make_async_remote_copy(
        src_ref=o_ref.at[got],
        dst_ref=o_ref.at[got],
        send_sem=s1.at[1],
        recv_sem=r1.at[1],
        device_id=twin,
        device_id_type=MESH,
    )
    beside.start()
    mine.wait()
    across.wait_send()
    beside.wait()


KINDS = ("all", "rows", "blk", "pair", "total", "move", "centres")


def params(kind):
    return pltpu.CompilerParams(collective_id=KINDS.index(kind), has_side_effects=True)


def vmem():
    return pl.BlockSpec(memory_space=pltpu.VMEM)


def summed(kind, nb, nr, width, x):
    n = nb * nr
    if n > 64 or nb != 2:
        if kind == "all":
            return lax.psum(x, ("blk", "rows"))
        if kind == "rows":
            return lax.all_gather(lax.psum(x, "rows"), "blk", axis=1, tiled=True)
        return lax.all_gather(lax.psum(x, "blk"), "rows", axis=1, tiled=True)
    parts = {"all": n, "rows": nr, "blk": nb}[kind]
    chunk = width // n
    dma = pltpu.SemaphoreType.DMA
    return pl.pallas_call(
        functools.partial(sum_kernel, kind, nb, nr),
        out_shape=jax.ShapeDtypeStruct((PAD, width), jnp.float32),
        in_specs=[vmem()],
        out_specs=vmem(),
        scratch_shapes=[
            pltpu.VMEM((parts, PAD, chunk), jnp.float32),
            pltpu.VMEM((PAD, width), jnp.float32),
            dma((parts,)),
            dma((parts,)),
            dma((n,)),
            dma((n,)),
        ],
        compiler_params=params(kind),
    )(x)


def swapped(kind, nb, nr, x):
    n = nb * nr
    if n > 64 or nb != 2:
        if kind == "pair":
            return lax.psum(x, "blk")
        if kind == "total":
            return lax.psum(x, ("blk", "rows"))
        return lax.all_to_all(x, "rows", split_axis=0, concat_axis=0, tiled=True)
    parts = {"pair": nb, "total": n, "move": nr}[kind]
    dma = pltpu.SemaphoreType.DMA
    land = x.shape if kind == "move" else (parts,) + x.shape
    return pl.pallas_call(
        functools.partial(swap_kernel, kind, nb, nr),
        out_shape=jax.ShapeDtypeStruct(x.shape, jnp.float32),
        in_specs=[vmem()],
        out_specs=vmem(),
        scratch_shapes=[pltpu.VMEM(land, jnp.float32), dma((parts,)), dma((parts,))],
        compiler_params=params(kind),
    )(x)


def all_centres(nb, nr, centres):
    if nb * nr > 64 or nb != 2 or nr % 2:
        return lax.all_gather(centres, "blk", axis=0, tiled=True)
    rows, width = centres.shape
    dma = pltpu.SemaphoreType.DMA
    anywhere = pl.BlockSpec(memory_space=pl.ANY)
    return pl.pallas_call(
        functools.partial(centre_kernel, nb, nr),
        out_shape=jax.ShapeDtypeStruct((nb * rows, width), centres.dtype),
        in_specs=[anywhere],
        out_specs=anywhere,
        scratch_shapes=[dma, dma((2,)), dma((2,))],
        compiler_params=params("centres"),
    )(centres)


def square_norms(rows_x):
    return jnp.einsum("nd,nd->n", rows_x, rows_x, preferred_element_type=jnp.float32)


def to_low(values):
    return lax.reduce_precision(values, 8, 7).astype(jnp.bfloat16)


def with_scalars(vector, scalars):
    return vector + jnp.pad(scalars[None, :], ((PAD - 1, 0), (0, vector.shape[1] - PAD)))


def on_device(nb, nr, features, labels, destination, centres, tri_inverse, aux_inverse):
    own_rows, width = features.shape
    block_rows, block_cols = tri_inverse.shape
    centre_count = block_rows * nb
    capacity = max(2, 2 * own_rows // nr)
    scale = 2.0 / width
    count_all = float(own_rows * nb * nr)
    b, r = lax.axis_index("blk"), lax.axis_index("rows")
    class_rows = jnp.arange(PAD, dtype=jnp.int32)[:, None]
    real = class_rows < CLASSES

    every_centre = all_centres(nb, nr, centres)
    centre_norm = square_norms(every_centre)
    rows_norm = square_norms(features)
    inner = lax.dot_general(
        features, every_centre, (((1,), (1,)), ((), ())), preferred_element_type=jnp.float32
    )
    kmat = jnp.exp(-(rows_norm[:, None] + centre_norm[None, :] - 2.0 * inner) * scale).astype(
        jnp.bfloat16
    )
    targets = jnp.where(
        real, jnp.where(labels[None, :] == class_rows, 1.0, -1.0), 0.0
    ).astype(jnp.bfloat16)

    def total_of(kind, x):
        return summed(kind, nb, nr, centre_count, x)

    def clean(vector):
        return jnp.where(real, vector, 0.0)

    def by_blk(vector):
        return lax.dynamic_slice_in_dim(vector, b * block_rows, block_rows, 1)

    def by_rows(vector):
        return lax.dynamic_slice_in_dim(vector, r * block_cols, block_cols, 1)

    def forward(block, ours):
        return lax.dot_general(
            ours, block, (((1,), (1,)), ((), ())), precision=highest, preferred_element_type=jnp.float32
        )

    def backward(block, ours):
        return jnp.dot(ours, block, precision=highest, preferred_element_type=jnp.float32)

    def onto_rows(low):
        return lax.dot_general(
            low, kmat, (((1,), (1,)), ((), ())), preferred_element_type=jnp.float32
        )

    def images(second):
        high = to_low(second)
        rest = second - high.astype(jnp.float32)
        mid = to_low(rest)
        low = to_low(rest - mid.astype(jnp.float32))
        three = onto_rows(jnp.concatenate([high, mid, low], axis=0))
        image = to_low(three[:PAD])
        exact = three[:PAD] + (three[PAD : 2 * PAD] + three[2 * PAD :])
        curve = jnp.sum(image.astype(jnp.float32) * exact, axis=1) / count_all
        return image, curve

    def ratio(above, below):
        return jnp.where(real, (above / below)[:, None], 0.0)

    def normal(vector):
        return jnp.sum(vector * vector, axis=1)

    start = total_of(
        "all", jnp.dot(targets, kmat, preferred_element_type=jnp.float32) / count_all
    )
    start = total_of("blk", backward(tri_inverse, by_blk(start)))
    rhs = swapped("pair", nb, nr, backward(aux_inverse, by_blk(start)))
    joined = total_of("rows", with_scalars(forward(aux_inverse, rhs), normal(rhs)))
    norm_first = joined[PAD - 1, :PAD]
    first = clean(joined)
    second = total_of("rows", forward(tri_inverse, by_rows(first)))
    image, curve = images(second)
    joined = total_of(
        "all",
        with_scalars(jnp.dot(image, kmat, preferred_element_type=jnp.float32) / count_all, curve),
    )
    step_first = ratio(norm_first, joined[PAD - 1, :PAD] + ridge_weight * normal(first))
    third = total_of("blk", backward(tri_inverse, by_blk(clean(joined))))
    turned = swapped(
        "pair", nb, nr, backward(aux_inverse, by_blk(third + ridge_weight * first))
    )
    residual = rhs - step_first * turned
    joined = total_of("rows", with_scalars(forward(aux_inverse, residual), normal(residual)))
    norm_next = joined[PAD - 1, :PAD]
    first_next = clean(joined) + ratio(norm_next, norm_first) * first
    second_next = total_of("rows", forward(tri_inverse, by_rows(first_next)))
    image, curve = images(second_next)
    curve = swapped("total", nb, nr, jnp.pad(curve[:, None], ((0, 0), (0, 127))))[:, 0]
    step_next = ratio(norm_next, curve + ridge_weight * normal(first_next))
    coefficients = step_first * second + step_next * second_next
    scores = onto_rows(to_low(coefficients))

    target = destination[:, 0]
    row_ids = jnp.arange(own_rows, dtype=jnp.int32)
    same = (target[:, None] == target[None, :]) & (row_ids[None, :] < row_ids[:, None])
    before = jnp.sum(same.astype(jnp.int32), axis=1)
    slots = nr * capacity
    spread = (
        (target * capacity + before)[:, None] == jnp.arange(slots, dtype=jnp.int32)[None, :]
    ).astype(jnp.float32)
    placed = jnp.dot(scores, spread, precision=highest, preferred_element_type=jnp.float32)
    placed = placed.reshape(PAD, nr, capacity).transpose(1, 0, 2)
    lanes = -capacity % 128
    moved = swapped("move", nb, nr, jnp.pad(placed, ((0, 0), (0, 0), (0, lanes))))
    moved = moved[:, :CLASSES, :capacity]
    return moved.transpose(1, 0, 2).reshape(CLASSES, slots)


def solution(mesh):
    return jax.shard_map(
        functools.partial(on_device, mesh.shape["blk"], mesh.shape["rows"]),
        mesh=mesh,
        in_specs=(
            P(("blk", "rows"), None),
            P(("blk", "rows")),
            P(("blk", "rows"), None),
            P("blk", None),
            P("blk", "rows"),
            P("blk", "rows"),
        ),
        out_specs=P(None, ("blk", "rows")),
        check_vma=False,
    )
```

```python
import functools

import jax
import jax.numpy as jnp
from jax import lax
from jax.experimental import pallas as pl
from jax.experimental.pallas import tpu as pltpu
from jax.sharding import PartitionSpec as P

CLASSES = 7
PAD = 8
MESH = pl.DeviceIdType.MESH
ridge_weight = 0.1
highest = lax.Precision.HIGHEST


def greet(peers, count):
    barrier = pltpu.get_barrier_semaphore()

    def hello(k, carry):
        pl.semaphore_signal(barrier, inc=1, device_id=peers(k), device_id_type=MESH)
        return carry

    lax.fori_loop(1, count, hello, 0)
    pl.semaphore_wait(barrier, count - 1)


def exchange(make, count, then):
    def send(k, carry):
        make(k).start()
        return carry

    def arrive(k, carry):
        make(k).wait_recv()
        return carry

    def left(k, carry):
        make(k).wait_send()
        return carry

    lax.fori_loop(1, count, send, 0)
    lax.fori_loop(1, count, arrive, 0)
    if then is not None:
        then()
    lax.fori_loop(1, count, left, 0)


def spot(index, chunk):
    return pl.ds(pl.multiple_of(index * chunk, chunk), chunk)


def add_parts(land):
    total = land[0]
    for index in range(1, land.shape[0]):
        total = total + land[index]
    return total


def spread_rows(nr, chunk, x_ref, land, s1, r1):
    b, r = lax.axis_index("blk"), lax.axis_index("rows")

    def make(k):
        other = lax.rem(r + k, nr)
        return pltpu.make_async_remote_copy(
            src_ref=x_ref.at[:, spot(other, chunk)],
            dst_ref=land.at[r],
            send_sem=s1.at[k],
            recv_sem=r1.at[k],
            device_id=(b, other),
            device_id_type=MESH,
        )

    land[r] = x_ref[:, spot(r, chunk)]
    return make


def plane_kernel(nb, nr, x_ref, o_ref, land, full, s1, r1, s2, r2):
    b, r = lax.axis_index("blk"), lax.axis_index("rows")
    chunk = land.shape[2]
    greet(lambda k: (b, lax.rem(r + k, nr)), nr)
    make = spread_rows(nr, chunk, x_ref, land, s1, r1)

    def add_up():
        full[:, spot(r, chunk)] = add_parts(land)

    exchange(make, nr, add_up)

    def gather(k):
        return pltpu.make_async_remote_copy(
            src_ref=full.at[:, spot(r, chunk)],
            dst_ref=full.at[:, spot(r, chunk)],
            send_sem=s2.at[k],
            recv_sem=r2.at[k],
            device_id=(b, lax.rem(r + k, nr)),
            device_id_type=MESH,
        )

    exchange(gather, nr, None)
    o_ref[...] = full[...]


def slice_kernel(nb, nr, x_ref, o_ref, land, mine, full, s1, r1, s2, r2):
    b, r = lax.axis_index("blk"), lax.axis_index("rows")
    me = b * nr + r
    chunk = land.shape[2]
    barrier = pltpu.get_barrier_semaphore()

    def hello(k, carry):
        pl.semaphore_signal(
            barrier, inc=1, device_id=(b, lax.rem(r + k, nr)), device_id_type=MESH
        )
        return carry

    lax.fori_loop(1, nr, hello, 0)
    for q in range(nb):
        source = r * nb + q

        @pl.when(source // nr != b)
        def _():
            pl.semaphore_signal(
                barrier,
                inc=1,
                device_id=(source // nr, lax.rem(source, nr)),
                device_id_type=MESH,
            )

    pl.semaphore_wait(barrier, nr - 1 + nb - 1)
    make = spread_rows(nr, chunk, x_ref, land, s1, r1)

    def add_up():
        mine[...] = add_parts(land)

    exchange(make, nr, add_up)
    taker, part = me // nb, lax.rem(me, nb)

    def deliver(q):
        return pltpu.make_async_remote_copy(
            src_ref=mine,
            dst_ref=full.at[:, spot(part, chunk)],
            send_sem=s2.at[q],
            recv_sem=r2.at[part],
            device_id=(q, taker),
            device_id_type=MESH,
        )

    def arrival(q):
        return pltpu.make_async_remote_copy(
            src_ref=mine,
            dst_ref=full.at[:, spot(q, chunk)],
            send_sem=s2.at[q],
            recv_sem=r2.at[q],
            device_id=(b, r),
            device_id_type=MESH,
        )

    for q in range(nb):
        own = q * nr + taker == me

        @pl.when(jnp.logical_not(own))
        def _():
            deliver(q).start()

        @pl.when(own)
        def _():
            full[:, spot(part, chunk)] = mine[...]

    for q in range(nb):

        @pl.when(r * nb + q != me)
        def _():
            arrival(q).wait_recv()

    for q in range(nb):

        @pl.when(q * nr + taker != me)
        def _():
            deliver(q).wait_send()

    o_ref[...] = full[...]


def turn_kernel(nb, nr, x_ref, add_ref, o_ref, land, mine, full, s1, r1, s2, r2):
    b, r = lax.axis_index("blk"), lax.axis_index("rows")
    me = b * nr + r
    chunk = land.shape[2]
    place = r * nb + b
    plane, part = place // nr, lax.rem(place, nr)
    barrier = pltpu.get_barrier_semaphore()
    for k in range(1, nb):
        pl.semaphore_signal(
            barrier, inc=1, device_id=(lax.rem(b + k, nb), r), device_id_type=MESH
        )

    def hello(p, carry):
        whose = b * nr + p
        side, line = lax.rem(whose, nb), whose // nb

        @pl.when(side * nr + line != me)
        def _():
            pl.semaphore_signal(barrier, inc=1, device_id=(side, line), device_id_type=MESH)

        return carry

    lax.fori_loop(0, nr, hello, 0)
    pl.semaphore_wait(barrier, nb - 1 + nr - (plane == b).astype(jnp.int32))

    def make(k):
        other = lax.rem(b + k, nb)
        return pltpu.make_async_remote_copy(
            src_ref=x_ref.at[:, spot(other, chunk)],
            dst_ref=land.at[b],
            send_sem=s1.at[k],
            recv_sem=r1.at[k],
            device_id=(other, r),
            device_id_type=MESH,
        )

    land[b] = x_ref[:, spot(b, chunk)]

    def add_up():
        mine[...] = add_parts(land) + add_ref[:, spot(b, chunk)]

    exchange(make, nb, add_up)

    def deliver(k):
        other = lax.rem(r + k, nr)
        return other, pltpu.make_async_remote_copy(
            src_ref=mine,
            dst_ref=full.at[:, spot(part, chunk)],
            send_sem=s2.at[k],
            recv_sem=r2.at[part],
            device_id=(plane, other),
            device_id_type=MESH,
        )

    def arrival(p):
        return pltpu.make_async_remote_copy(
            src_ref=mine,
            dst_ref=full.at[:, spot(p, chunk)],
            send_sem=s2.at[p],
            recv_sem=r2.at[p],
            device_id=(b, r),
            device_id_type=MESH,
        )

    def start(k, carry):
        deliver(k)[1].start()
        return carry

    def arrive(p, carry):
        whose = b * nr + p

        @pl.when(lax.rem(whose, nb) * nr + whose // nb != me)
        def _():
            arrival(p).wait_recv()

        return carry

    def left(k, carry):
        deliver(k)[1].wait_send()
        return carry

    @pl.when(plane != b)
    def _():
        deliver(0)[1].start()

    lax.fori_loop(1, nr, start, 0)

    @pl.when(plane == b)
    def _():
        full[:, spot(part, chunk)] = mine[...]

    lax.fori_loop(0, nr, arrive, 0)

    @pl.when(plane != b)
    def _():
        deliver(0)[1].wait_send()

    lax.fori_loop(1, nr, left, 0)
    o_ref[...] = full[...]


def swap_kernel(kind, nb, nr, x_ref, o_ref, land, s1, r1):
    b, r = lax.axis_index("blk"), lax.axis_index("rows")
    across = kind in ("pair", "images", "share")
    parts, own = (nb, b) if across else (nr, r)

    def device(k):
        other = lax.rem(own + k, parts)
        return (other, r) if across else (b, other)

    greet(device, parts)

    def make(k):
        source = x_ref.at[lax.rem(own + k, parts)] if kind == "move" else x_ref
        return pltpu.make_async_remote_copy(
            src_ref=source,
            dst_ref=land.at[own],
            send_sem=s1.at[k],
            recv_sem=r1.at[k],
            device_id=device(k),
            device_id_type=MESH,
        )

    land[own] = x_ref[own] if kind == "move" else x_ref[...]

    def finish():
        o_ref[...] = land[...] if kind in ("move", "share") else add_parts(land)

    exchange(make, parts, finish)


KINDS = ("plane", "slice", "turn", "pair", "images", "share", "total", "move")


def call(kind, body, nb, nr, shape, dtype, scratch, *operands):
    whole = pl.BlockSpec(memory_space=pltpu.VMEM)
    return pl.pallas_call(
        functools.partial(body, nb, nr),
        out_shape=jax.ShapeDtypeStruct(shape, dtype),
        in_specs=[whole] * len(operands),
        out_specs=whole,
        scratch_shapes=scratch,
        compiler_params=pltpu.CompilerParams(
            collective_id=KINDS.index(kind), has_side_effects=True
        ),
    )(*operands)


def plain(nb, nr):
    return nb * nr > 64 or nb != 2


dma = pltpu.SemaphoreType.DMA


def float_buffer(*shape):
    return pltpu.VMEM(shape, jnp.float32)


def plane_sum(nb, nr, x):
    if plain(nb, nr):
        return lax.psum(x, "rows")
    width = x.shape[1]
    scratch = [float_buffer(nr, PAD, width // nr), float_buffer(PAD, width)] + [dma((nr,))] * 4
    return call("plane", plane_kernel, nb, nr, x.shape, jnp.float32, scratch, x)


def slice_sum(nb, nr, x):
    size = x.shape[1] * nb // nr
    if plain(nb, nr):
        full = lax.all_gather(lax.psum(x, "rows"), "blk", axis=1, tiled=True)
        return lax.dynamic_slice_in_dim(full, lax.axis_index("rows") * size, size, 1)
    chunk = x.shape[1] // nr
    scratch = [
        float_buffer(nr, PAD, chunk),
        float_buffer(PAD, chunk),
        float_buffer(PAD, size),
        dma((nr,)),
        dma((nr,)),
        dma((nb,)),
        dma((nb,)),
    ]
    return call("slice", slice_kernel, nb, nr, (PAD, size), jnp.float32, scratch, x)


def turn_sum(nb, nr, x, add):
    width = x.shape[1] * nr // nb
    if plain(nb, nr):
        full = lax.all_gather(lax.psum(x, "blk") + add, "rows", axis=1, tiled=True)
        return lax.dynamic_slice_in_dim(full, lax.axis_index("blk") * width, width, 1)
    chunk = x.shape[1] // nb
    scratch = [
        float_buffer(nb, PAD, chunk),
        float_buffer(PAD, chunk),
        float_buffer(PAD, width),
        dma((nb,)),
        dma((nb,)),
        dma((nr,)),
        dma((nr,)),
    ]
    return call("turn", turn_kernel, nb, nr, (PAD, width), jnp.float32, scratch, x, add)


def swapped(kind, nb, nr, x):
    if plain(nb, nr):
        if kind == "total":
            return lax.psum(x, "rows")
        if kind == "move":
            return lax.all_to_all(x, "rows", split_axis=0, concat_axis=0, tiled=True)
        if kind == "share":
            return lax.all_gather(x, "blk", axis=0)
        return lax.psum(x, "blk")
    parts = nr if kind in ("total", "move") else nb
    land = x.shape if kind == "move" else (parts,) + x.shape
    shape = land if kind == "share" else x.shape
    scratch = [pltpu.VMEM(land, x.dtype), dma((parts,)), dma((parts,))]
    return call(kind, functools.partial(swap_kernel, kind), nb, nr, shape, x.dtype, scratch, x)


def square_norms(rows_x):
    return jnp.einsum("nd,nd->n", rows_x, rows_x, preferred_element_type=jnp.float32)


def to_low(values):
    return lax.reduce_precision(values, 8, 7).astype(jnp.bfloat16)


def with_scalars(vector, scalars):
    return vector + jnp.pad(scalars[None, :], ((PAD - 1, 0), (0, vector.shape[1] - PAD)))


def on_device(nb, nr, features, labels, destination, centres, tri_inverse, aux_inverse):
    own_rows, width = features.shape
    capacity = max(2, 2 * own_rows // nr)
    scale = 2.0 / width
    count_all = float(own_rows * nb * nr)
    b = lax.axis_index("blk")
    class_rows = jnp.arange(PAD, dtype=jnp.int32)[:, None]
    real = class_rows < CLASSES

    tags = jnp.pad(labels.astype(jnp.bfloat16), (0, -own_rows % (16 * width)))
    tags = tags.reshape(-1, width)
    shared = swapped("share", nb, nr, jnp.concatenate([features, tags], axis=0))
    rows_x = shared[:, :own_rows].reshape(nb * own_rows, width)
    tags = shared[:, own_rows:].reshape(nb, -1)[:, :own_rows].reshape(nb * own_rows)
    centre_norm = square_norms(centres)
    rows_norm = square_norms(rows_x)
    inner = lax.dot_general(
        rows_x, centres, (((1,), (1,)), ((), ())), preferred_element_type=jnp.float32
    )
    kmat = jnp.exp(-(rows_norm[:, None] + centre_norm[None, :] - 2.0 * inner) * scale).astype(
        jnp.bfloat16
    )
    hits = tags.astype(jnp.float32)[None, :] == class_rows.astype(jnp.float32)
    targets = jnp.where(real, jnp.where(hits, 1.0, -1.0), 0.0).astype(jnp.bfloat16)

    def clean(vector):
        return jnp.where(real, vector, 0.0)

    def forward(block, ours):
        return lax.dot_general(
            ours, block, (((1,), (1,)), ((), ())), precision=highest, preferred_element_type=jnp.float32
        )

    def backward(block, ours):
        return jnp.dot(ours, block, precision=highest, preferred_element_type=jnp.float32)

    def onto_rows(low):
        return lax.dot_general(
            low, kmat, (((1,), (1,)), ((), ())), preferred_element_type=jnp.float32
        )

    def images(second):
        high = to_low(second)
        rest = second - high.astype(jnp.float32)
        mid = to_low(rest)
        low = to_low(rest - mid.astype(jnp.float32))
        three = onto_rows(jnp.concatenate([high, mid, low], axis=0))
        both = jnp.concatenate([three[:PAD], three[PAD : 2 * PAD] + three[2 * PAD :]], axis=0)
        both = swapped("images", nb, nr, both)
        image = to_low(both[:PAD])
        exact = both[:PAD] + both[PAD:]
        curve = jnp.sum(image.astype(jnp.float32) * exact, axis=1) / count_all
        return image, curve

    def ratio(above, below):
        return jnp.where(real, (above / below)[:, None], 0.0)

    def normal(vector):
        return jnp.sum(vector * vector, axis=1)

    start = plane_sum(nb, nr, jnp.dot(targets, kmat, preferred_element_type=jnp.float32) / count_all)
    start = backward(tri_inverse, start)
    start = turn_sum(nb, nr, start, jnp.zeros_like(start))
    rhs = swapped("pair", nb, nr, backward(aux_inverse, start))
    first = slice_sum(nb, nr, forward(aux_inverse, rhs))
    joined = plane_sum(nb, nr, with_scalars(forward(tri_inverse, first), normal(rhs)))
    norm_first = joined[PAD - 1, :PAD]
    second = clean(joined)
    image, curve = images(second)
    curve = curve + ridge_weight * normal(first)
    gram = jnp.dot(image, kmat, preferred_element_type=jnp.float32) / count_all
    joined = plane_sum(nb, nr, with_scalars(gram, curve))
    step_first = ratio(norm_first, joined[PAD - 1, :PAD])
    third = turn_sum(nb, nr, backward(tri_inverse, clean(joined)), ridge_weight * first)
    turned = swapped("pair", nb, nr, backward(aux_inverse, third))
    residual = rhs - step_first * turned
    first_next = slice_sum(nb, nr, forward(aux_inverse, residual))
    joined = plane_sum(nb, nr, with_scalars(forward(tri_inverse, first_next), normal(residual)))
    norm_next = joined[PAD - 1, :PAD]
    turn_weight = ratio(norm_next, norm_first)
    first_next = first_next + turn_weight * first
    second_next = clean(joined) + turn_weight * second
    image, curve = images(second_next)
    curve = curve + ridge_weight * normal(first_next)
    curve = swapped("total", nb, nr, jnp.pad(curve[:, None], ((0, 0), (0, 127))))[:, 0]
    step_next = ratio(norm_next, curve)
    coefficients = step_first * second + step_next * second_next
    scores = swapped("pair", nb, nr, onto_rows(to_low(coefficients)))
    scores = lax.dynamic_slice_in_dim(scores, b * own_rows, own_rows, 1)

    target = destination[:, 0]
    row_ids = jnp.arange(own_rows, dtype=jnp.int32)
    same = (target[:, None] == target[None, :]) & (row_ids[None, :] < row_ids[:, None])
    before = jnp.sum(same.astype(jnp.int32), axis=1)
    slots = nr * capacity
    spread = (
        (target * capacity + before)[:, None] == jnp.arange(slots, dtype=jnp.int32)[None, :]
    ).astype(jnp.float32)
    placed = jnp.dot(scores, spread, precision=highest, preferred_element_type=jnp.float32)
    placed = placed.reshape(PAD, nr, capacity).transpose(1, 0, 2)
    lanes = -capacity % 128
    moved = swapped("move", nb, nr, jnp.pad(placed, ((0, 0), (0, 0), (0, lanes))))
    moved = moved[:, :CLASSES, :capacity]
    return moved.transpose(1, 0, 2).reshape(CLASSES, slots)


def solution(mesh):
    return jax.shard_map(
        functools.partial(on_device, mesh.shape["blk"], mesh.shape["rows"]),
        mesh=mesh,
        in_specs=(
            P(("blk", "rows"), None),
            P(("blk", "rows")),
            P(("blk", "rows"), None),
            P("blk", None),
            P("blk", "rows"),
            P("blk", "rows"),
        ),
        out_specs=P(None, ("blk", "rows")),
        check_vma=False,
    )
```

```python
import functools

import jax
import jax.numpy as jnp
from jax import lax
from jax.experimental import pallas as pl
from jax.experimental.pallas import tpu as pltpu
from jax.sharding import PartitionSpec as P

CLASSES = 7
PAD = 8
MESH = pl.DeviceIdType.MESH
ridge_weight = 0.1
highest = lax.Precision.HIGHEST


def greet(peers, count):
    barrier = pltpu.get_barrier_semaphore()

    def hello(k, carry):
        pl.semaphore_signal(barrier, inc=1, device_id=peers(k), device_id_type=MESH)
        return carry

    lax.fori_loop(1, count, hello, 0)
    pl.semaphore_wait(barrier, count - 1)


def exchange(make, count, then):
    def send(k, carry):
        make(k).start()
        return carry

    def arrive(k, carry):
        make(k).wait_recv()
        return carry

    def left(k, carry):
        make(k).wait_send()
        return carry

    lax.fori_loop(1, count, send, 0)
    lax.fori_loop(1, count, arrive, 0)
    if then is not None:
        then()
    lax.fori_loop(1, count, left, 0)


def spot(index, chunk):
    return pl.ds(pl.multiple_of(index * chunk, chunk), chunk)


def add_parts(land):
    total = land[0]
    for index in range(1, land.shape[0]):
        total = total + land[index]
    return total


def spread_rows(nr, chunk, x_ref, land, s1, r1):
    b, r = lax.axis_index("blk"), lax.axis_index("rows")

    def make(k):
        other = lax.rem(r + k, nr)
        return pltpu.make_async_remote_copy(
            src_ref=x_ref.at[:, spot(other, chunk)],
            dst_ref=land.at[r],
            send_sem=s1.at[k],
            recv_sem=r1.at[k],
            device_id=(b, other),
            device_id_type=MESH,
        )

    land[r] = x_ref[:, spot(r, chunk)]
    return make


def plane_kernel(nb, nr, x_ref, o_ref, land, full, s1, r1, s2, r2):
    b, r = lax.axis_index("blk"), lax.axis_index("rows")
    chunk = land.shape[2]
    greet(lambda k: (b, lax.rem(r + k, nr)), nr)
    make = spread_rows(nr, chunk, x_ref, land, s1, r1)

    def add_up():
        full[:, spot(r, chunk)] = add_parts(land)

    exchange(make, nr, add_up)

    def gather(k):
        return pltpu.make_async_remote_copy(
            src_ref=full.at[:, spot(r, chunk)],
            dst_ref=full.at[:, spot(r, chunk)],
            send_sem=s2.at[k],
            recv_sem=r2.at[k],
            device_id=(b, lax.rem(r + k, nr)),
            device_id_type=MESH,
        )

    exchange(gather, nr, None)
    o_ref[...] = full[...]


def slice_kernel(nb, nr, x_ref, o_ref, land, mine, full, s1, r1, s2, r2):
    b, r = lax.axis_index("blk"), lax.axis_index("rows")
    me = b * nr + r
    chunk = land.shape[2]
    barrier = pltpu.get_barrier_semaphore()

    def hello(k, carry):
        pl.semaphore_signal(
            barrier, inc=1, device_id=(b, lax.rem(r + k, nr)), device_id_type=MESH
        )
        return carry

    lax.fori_loop(1, nr, hello, 0)
    for q in range(nb):
        source = r * nb + q

        @pl.when(source // nr != b)
        def _():
            pl.semaphore_signal(
                barrier,
                inc=1,
                device_id=(source // nr, lax.rem(source, nr)),
                device_id_type=MESH,
            )

    pl.semaphore_wait(barrier, nr - 1 + nb - 1)
    make = spread_rows(nr, chunk, x_ref, land, s1, r1)

    def add_up():
        mine[...] = add_parts(land)

    exchange(make, nr, add_up)
    taker, part = me // nb, lax.rem(me, nb)

    def deliver(q):
        return pltpu.make_async_remote_copy(
            src_ref=mine,
            dst_ref=full.at[:, spot(part, chunk)],
            send_sem=s2.at[q],
            recv_sem=r2.at[part],
            device_id=(q, taker),
            device_id_type=MESH,
        )

    def arrival(q):
        return pltpu.make_async_remote_copy(
            src_ref=mine,
            dst_ref=full.at[:, spot(q, chunk)],
            send_sem=s2.at[q],
            recv_sem=r2.at[q],
            device_id=(b, r),
            device_id_type=MESH,
        )

    for q in range(nb):
        own = q * nr + taker == me

        @pl.when(jnp.logical_not(own))
        def _():
            deliver(q).start()

        @pl.when(own)
        def _():
            full[:, spot(part, chunk)] = mine[...]

    for q in range(nb):

        @pl.when(r * nb + q != me)
        def _():
            arrival(q).wait_recv()

    for q in range(nb):

        @pl.when(q * nr + taker != me)
        def _():
            deliver(q).wait_send()

    o_ref[...] = full[...]


def turn_kernel(nb, nr, x_ref, add_ref, o_ref, land, mine, full, s1, r1, s2, r2):
    b, r = lax.axis_index("blk"), lax.axis_index("rows")
    me = b * nr + r
    chunk = land.shape[2]
    place = r * nb + b
    plane, part = place // nr, lax.rem(place, nr)
    barrier = pltpu.get_barrier_semaphore()
    for k in range(1, nb):
        pl.semaphore_signal(
            barrier, inc=1, device_id=(lax.rem(b + k, nb), r), device_id_type=MESH
        )

    def hello(p, carry):
        whose = b * nr + p
        side, line = lax.rem(whose, nb), whose // nb

        @pl.when(side * nr + line != me)
        def _():
            pl.semaphore_signal(barrier, inc=1, device_id=(side, line), device_id_type=MESH)

        return carry

    lax.fori_loop(0, nr, hello, 0)
    pl.semaphore_wait(barrier, nb - 1 + nr - (plane == b).astype(jnp.int32))

    def make(k):
        other = lax.rem(b + k, nb)
        return pltpu.make_async_remote_copy(
            src_ref=x_ref.at[:, spot(other, chunk)],
            dst_ref=land.at[b],
            send_sem=s1.at[k],
            recv_sem=r1.at[k],
            device_id=(other, r),
            device_id_type=MESH,
        )

    land[b] = x_ref[:, spot(b, chunk)]

    def add_up():
        mine[...] = add_parts(land) + add_ref[:, spot(b, chunk)]

    exchange(make, nb, add_up)

    def deliver(k):
        other = lax.rem(r + k, nr)
        return other, pltpu.make_async_remote_copy(
            src_ref=mine,
            dst_ref=full.at[:, spot(part, chunk)],
            send_sem=s2.at[k],
            recv_sem=r2.at[part],
            device_id=(plane, other),
            device_id_type=MESH,
        )

    def arrival(p):
        return pltpu.make_async_remote_copy(
            src_ref=mine,
            dst_ref=full.at[:, spot(p, chunk)],
            send_sem=s2.at[p],
            recv_sem=r2.at[p],
            device_id=(b, r),
            device_id_type=MESH,
        )

    def start(k, carry):
        deliver(k)[1].start()
        return carry

    def arrive(p, carry):
        whose = b * nr + p

        @pl.when(lax.rem(whose, nb) * nr + whose // nb != me)
        def _():
            arrival(p).wait_recv()

        return carry

    def left(k, carry):
        deliver(k)[1].wait_send()
        return carry

    @pl.when(plane != b)
    def _():
        deliver(0)[1].start()

    lax.fori_loop(1, nr, start, 0)

    @pl.when(plane == b)
    def _():
        full[:, spot(part, chunk)] = mine[...]

    lax.fori_loop(0, nr, arrive, 0)

    @pl.when(plane != b)
    def _():
        deliver(0)[1].wait_send()

    lax.fori_loop(1, nr, left, 0)
    o_ref[...] = full[...]


def swap_kernel(kind, nb, nr, x_ref, o_ref, land, s1, r1):
    b, r = lax.axis_index("blk"), lax.axis_index("rows")
    across = kind in ("pair", "images", "share")
    parts, own = (nb, b) if across else (nr, r)

    def device(k):
        other = lax.rem(own + k, parts)
        return (other, r) if across else (b, other)

    greet(device, parts)

    def make(k):
        source = x_ref.at[lax.rem(own + k, parts)] if kind == "move" else x_ref
        return pltpu.make_async_remote_copy(
            src_ref=source,
            dst_ref=land.at[own],
            send_sem=s1.at[k],
            recv_sem=r1.at[k],
            device_id=device(k),
            device_id_type=MESH,
        )

    land[own] = x_ref[own] if kind == "move" else x_ref[...]

    def finish():
        o_ref[...] = land[...] if kind in ("move", "share") else add_parts(land)

    exchange(make, parts, finish)


KINDS = ("plane", "slice", "turn", "pair", "images", "share", "total", "move")


def call(kind, body, nb, nr, shape, dtype, scratch, *operands):
    whole = pl.BlockSpec(memory_space=pltpu.VMEM)
    return pl.pallas_call(
        functools.partial(body, nb, nr),
        out_shape=jax.ShapeDtypeStruct(shape, dtype),
        in_specs=[whole] * len(operands),
        out_specs=whole,
        scratch_shapes=scratch,
        compiler_params=pltpu.CompilerParams(
            collective_id=KINDS.index(kind), has_side_effects=True
        ),
    )(*operands)


def plain(nb, nr):
    return nb * nr > 64 or nb != 2


dma = pltpu.SemaphoreType.DMA


def float_buffer(*shape):
    return pltpu.VMEM(shape, jnp.float32)


def plane_sum(nb, nr, x):
    if plain(nb, nr):
        return lax.psum(x, "rows")
    width = x.shape[1]
    scratch = [float_buffer(nr, PAD, width // nr), float_buffer(PAD, width)] + [dma((nr,))] * 4
    return call("plane", plane_kernel, nb, nr, x.shape, jnp.float32, scratch, x)


def slice_sum(nb, nr, x):
    size = x.shape[1] * nb // nr
    if plain(nb, nr):
        full = lax.all_gather(lax.psum(x, "rows"), "blk", axis=1, tiled=True)
        return lax.dynamic_slice_in_dim(full, lax.axis_index("rows") * size, size, 1)
    chunk = x.shape[1] // nr
    scratch = [
        float_buffer(nr, PAD, chunk),
        float_buffer(PAD, chunk),
        float_buffer(PAD, size),
        dma((nr,)),
        dma((nr,)),
        dma((nb,)),
        dma((nb,)),
    ]
    return call("slice", slice_kernel, nb, nr, (PAD, size), jnp.float32, scratch, x)


def turn_sum(nb, nr, x, add):
    width = x.shape[1] * nr // nb
    if plain(nb, nr):
        full = lax.all_gather(lax.psum(x, "blk") + add, "rows", axis=1, tiled=True)
        return lax.dynamic_slice_in_dim(full, lax.axis_index("blk") * width, width, 1)
    chunk = x.shape[1] // nb
    scratch = [
        float_buffer(nb, PAD, chunk),
        float_buffer(PAD, chunk),
        float_buffer(PAD, width),
        dma((nb,)),
        dma((nb,)),
        dma((nr,)),
        dma((nr,)),
    ]
    return call("turn", turn_kernel, nb, nr, (PAD, width), jnp.float32, scratch, x, add)


def swapped(kind, nb, nr, x):
    if plain(nb, nr):
        if kind == "total":
            return lax.psum(x, "rows")
        if kind == "move":
            return lax.all_to_all(x, "rows", split_axis=0, concat_axis=0, tiled=True)
        if kind == "share":
            return lax.all_gather(x, "blk", axis=0)
        return lax.psum(x, "blk")
    parts = nr if kind in ("total", "move") else nb
    land = x.shape if kind == "move" else (parts,) + x.shape
    shape = land if kind == "share" else x.shape
    scratch = [pltpu.VMEM(land, x.dtype), dma((parts,)), dma((parts,))]
    return call(kind, functools.partial(swap_kernel, kind), nb, nr, shape, x.dtype, scratch, x)


def three_parts(x):
    high = x.astype(jnp.bfloat16).astype(jnp.float32)
    rest = x - high
    mid = rest.astype(jnp.bfloat16).astype(jnp.float32)
    return high, mid, rest - mid


def exact_product(dims, vector, block):
    stacked = jnp.concatenate(three_parts(vector), axis=0).astype(jnp.bfloat16)
    total = None
    for part in reversed(three_parts(block)):
        product = lax.dot_general(
            stacked, part.astype(jnp.bfloat16), dims, preferred_element_type=jnp.float32
        )
        product = product[2 * PAD :] + product[PAD : 2 * PAD] + product[:PAD]
        total = product if total is None else total + product
    return total


def forward_kernel(u_ref, block_ref, o_ref):
    o_ref[...] = exact_product((((1,), (1,)), ((), ())), u_ref[...], block_ref[...])


def backward_kernel(u_ref, block_ref, o_ref):
    product = exact_product((((1,), (0,)), ((), ())), u_ref[...], block_ref[...])

    @pl.when(pl.program_id(0) == 0)
    def _():
        o_ref[...] = product

    @pl.when(pl.program_id(0) > 0)
    def _():
        o_ref[...] += product


STEP = 512


def factor_forward(block, vector):
    rows, cols = block.shape
    return pl.pallas_call(
        forward_kernel,
        grid=(rows // STEP,),
        in_specs=[
            pl.BlockSpec((PAD, cols), lambda i: (0, 0)),
            pl.BlockSpec((STEP, cols), lambda i: (i, 0)),
        ],
        out_specs=pl.BlockSpec((PAD, STEP), lambda i: (0, i)),
        out_shape=jax.ShapeDtypeStruct((PAD, rows), jnp.float32),
    )(vector, block)


def factor_backward(block, vector):
    rows, cols = block.shape
    return pl.pallas_call(
        backward_kernel,
        grid=(rows // STEP,),
        in_specs=[
            pl.BlockSpec((PAD, STEP), lambda i: (0, i)),
            pl.BlockSpec((STEP, cols), lambda i: (i, 0)),
        ],
        out_specs=pl.BlockSpec((PAD, cols), lambda i: (0, 0)),
        out_shape=jax.ShapeDtypeStruct((PAD, cols), jnp.float32),
    )(vector, block)


def square_norms(rows_x):
    return jnp.einsum("nd,nd->n", rows_x, rows_x, preferred_element_type=jnp.float32)


def to_low(values):
    return lax.reduce_precision(values, 8, 7).astype(jnp.bfloat16)


def with_scalars(vector, scalars):
    return vector + jnp.pad(scalars[None, :], ((PAD - 1, 0), (0, vector.shape[1] - PAD)))


def on_device(nb, nr, features, labels, destination, centres, tri_inverse, aux_inverse):
    own_rows, width = features.shape
    capacity = max(2, 2 * own_rows // nr)
    scale = 2.0 / width
    count_all = float(own_rows * nb * nr)
    b = lax.axis_index("blk")
    class_rows = jnp.arange(PAD, dtype=jnp.int32)[:, None]
    real = class_rows < CLASSES

    tags = jnp.pad(labels.astype(jnp.bfloat16), (0, -own_rows % (16 * width)))
    tags = tags.reshape(-1, width)
    shared = swapped("share", nb, nr, jnp.concatenate([features, tags], axis=0))
    rows_x = shared[:, :own_rows].reshape(nb * own_rows, width)
    tags = shared[:, own_rows:].reshape(nb, -1)[:, :own_rows].reshape(nb * own_rows)
    centre_norm = square_norms(centres)
    rows_norm = square_norms(rows_x)
    inner = lax.dot_general(
        rows_x, centres, (((1,), (1,)), ((), ())), preferred_element_type=jnp.float32
    )
    kmat = jnp.exp(-(rows_norm[:, None] + centre_norm[None, :] - 2.0 * inner) * scale).astype(
        jnp.bfloat16
    )
    hits = tags.astype(jnp.float32)[None, :] == class_rows.astype(jnp.float32)
    targets = jnp.where(real, jnp.where(hits, 1.0, -1.0), 0.0).astype(jnp.bfloat16)

    def clean(vector):
        return jnp.where(real, vector, 0.0)

    def onto_rows(low):
        return lax.dot_general(
            low, kmat, (((1,), (1,)), ((), ())), preferred_element_type=jnp.float32
        )

    def images(second):
        high = to_low(second)
        rest = second - high.astype(jnp.float32)
        mid = to_low(rest)
        low = to_low(rest - mid.astype(jnp.float32))
        three = onto_rows(jnp.concatenate([high, mid, low], axis=0))
        both = jnp.concatenate([three[:PAD], three[PAD : 2 * PAD] + three[2 * PAD :]], axis=0)
        both = swapped("images", nb, nr, both)
        image = to_low(both[:PAD])
        exact = both[:PAD] + both[PAD:]
        curve = jnp.sum(image.astype(jnp.float32) * exact, axis=1) / count_all
        return image, curve

    def ratio(above, below):
        return jnp.where(real, (above / below)[:, None], 0.0)

    def normal(vector):
        return jnp.sum(vector * vector, axis=1)

    start = plane_sum(nb, nr, jnp.dot(targets, kmat, preferred_element_type=jnp.float32) / count_all)
    start = factor_backward(tri_inverse, start)
    start = turn_sum(nb, nr, start, jnp.zeros_like(start))
    rhs = swapped("pair", nb, nr, factor_backward(aux_inverse, start))
    first = slice_sum(nb, nr, factor_forward(aux_inverse, rhs))
    joined = plane_sum(nb, nr, with_scalars(factor_forward(tri_inverse, first), normal(rhs)))
    norm_first = joined[PAD - 1, :PAD]
    second = clean(joined)
    image, curve = images(second)
    curve = curve + ridge_weight * normal(first)
    gram = jnp.dot(image, kmat, preferred_element_type=jnp.float32) / count_all
    joined = plane_sum(nb, nr, with_scalars(gram, curve))
    step_first = ratio(norm_first, joined[PAD - 1, :PAD])
    third = turn_sum(nb, nr, factor_backward(tri_inverse, clean(joined)), ridge_weight * first)
    turned = swapped("pair", nb, nr, factor_backward(aux_inverse, third))
    residual = rhs - step_first * turned
    first_next = slice_sum(nb, nr, factor_forward(aux_inverse, residual))
    joined = plane_sum(nb, nr, with_scalars(factor_forward(tri_inverse, first_next), normal(residual)))
    norm_next = joined[PAD - 1, :PAD]
    turn_weight = ratio(norm_next, norm_first)
    first_next = first_next + turn_weight * first
    second_next = clean(joined) + turn_weight * second
    image, curve = images(second_next)
    curve = curve + ridge_weight * normal(first_next)
    curve = swapped("total", nb, nr, jnp.pad(curve[:, None], ((0, 0), (0, 127))))[:, 0]
    step_next = ratio(norm_next, curve)
    coefficients = step_first * second + step_next * second_next
    scores = swapped("pair", nb, nr, onto_rows(to_low(coefficients)))
    scores = lax.dynamic_slice_in_dim(scores, b * own_rows, own_rows, 1)

    target = destination[:, 0]
    row_ids = jnp.arange(own_rows, dtype=jnp.int32)
    same = (target[:, None] == target[None, :]) & (row_ids[None, :] < row_ids[:, None])
    before = jnp.sum(same.astype(jnp.int32), axis=1)
    slots = nr * capacity
    spread = (
        (target * capacity + before)[:, None] == jnp.arange(slots, dtype=jnp.int32)[None, :]
    ).astype(jnp.float32)
    placed = jnp.dot(scores, spread, precision=highest, preferred_element_type=jnp.float32)
    placed = placed.reshape(PAD, nr, capacity).transpose(1, 0, 2)
    lanes = -capacity % 128
    moved = swapped("move", nb, nr, jnp.pad(placed, ((0, 0), (0, 0), (0, lanes))))
    moved = moved[:, :CLASSES, :capacity]
    return moved.transpose(1, 0, 2).reshape(CLASSES, slots)


def solution(mesh):
    return jax.shard_map(
        functools.partial(on_device, mesh.shape["blk"], mesh.shape["rows"]),
        mesh=mesh,
        in_specs=(
            P(("blk", "rows"), None),
            P(("blk", "rows")),
            P(("blk", "rows"), None),
            P("blk", None),
            P("blk", "rows"),
            P("blk", "rows"),
        ),
        out_specs=P(None, ("blk", "rows")),
        check_vma=False,
    )
```

```python
import functools

import jax
import jax.numpy as jnp
from jax import lax
from jax.experimental import pallas as pl
from jax.experimental.pallas import tpu as pltpu
from jax.sharding import PartitionSpec as P

CLASSES = 7
PAD = 8
MESH = pl.DeviceIdType.MESH
ridge_weight = 0.1
highest = lax.Precision.HIGHEST


def greet(peers, count):
    barrier = pltpu.get_barrier_semaphore()

    def hello(k, carry):
        pl.semaphore_signal(barrier, inc=1, device_id=peers(k), device_id_type=MESH)
        return carry

    lax.fori_loop(1, count, hello, 0)
    pl.semaphore_wait(barrier, count - 1)


def exchange(make, count, then):
    def send(k, carry):
        make(k).start()
        return carry

    def arrive(k, carry):
        make(k).wait_recv()
        return carry

    def left(k, carry):
        make(k).wait_send()
        return carry

    lax.fori_loop(1, count, send, 0)
    lax.fori_loop(1, count, arrive, 0)
    if then is not None:
        then()
    lax.fori_loop(1, count, left, 0)


def spot(index, chunk):
    return pl.ds(pl.multiple_of(index * chunk, chunk), chunk)


def add_parts(land):
    total = land[0]
    for index in range(1, land.shape[0]):
        total = total + land[index]
    return total


def spread_rows(nr, chunk, x_ref, land, s1, r1):
    b, r = lax.axis_index("blk"), lax.axis_index("rows")

    def make(k):
        other = lax.rem(r + k, nr)
        return pltpu.make_async_remote_copy(
            src_ref=x_ref.at[:, spot(other, chunk)],
            dst_ref=land.at[r],
            send_sem=s1.at[k],
            recv_sem=r1.at[k],
            device_id=(b, other),
            device_id_type=MESH,
        )

    land[r] = x_ref[:, spot(r, chunk)]
    return make


def plane_kernel(nb, nr, x_ref, o_ref, land, full, s1, r1, s2, r2):
    b, r = lax.axis_index("blk"), lax.axis_index("rows")
    chunk = land.shape[2]
    greet(lambda k: (b, lax.rem(r + k, nr)), nr)
    make = spread_rows(nr, chunk, x_ref, land, s1, r1)

    def add_up():
        full[:, spot(r, chunk)] = add_parts(land)

    exchange(make, nr, add_up)

    def gather(k):
        return pltpu.make_async_remote_copy(
            src_ref=full.at[:, spot(r, chunk)],
            dst_ref=full.at[:, spot(r, chunk)],
            send_sem=s2.at[k],
            recv_sem=r2.at[k],
            device_id=(b, lax.rem(r + k, nr)),
            device_id_type=MESH,
        )

    exchange(gather, nr, None)
    o_ref[...] = full[...]


def slice_kernel(nb, nr, x_ref, o_ref, land, mine, full, s1, r1, s2, r2):
    b, r = lax.axis_index("blk"), lax.axis_index("rows")
    me = b * nr + r
    chunk = land.shape[2]
    barrier = pltpu.get_barrier_semaphore()

    def hello(k, carry):
        pl.semaphore_signal(
            barrier, inc=1, device_id=(b, lax.rem(r + k, nr)), device_id_type=MESH
        )
        return carry

    lax.fori_loop(1, nr, hello, 0)
    for q in range(nb):
        source = r * nb + q

        @pl.when(source // nr != b)
        def _():
            pl.semaphore_signal(
                barrier,
                inc=1,
                device_id=(source // nr, lax.rem(source, nr)),
                device_id_type=MESH,
            )

    pl.semaphore_wait(barrier, nr - 1 + nb - 1)
    make = spread_rows(nr, chunk, x_ref, land, s1, r1)

    def add_up():
        mine[...] = add_parts(land)

    exchange(make, nr, add_up)
    taker, part = me // nb, lax.rem(me, nb)

    def deliver(q):
        return pltpu.make_async_remote_copy(
            src_ref=mine,
            dst_ref=full.at[:, spot(part, chunk)],
            send_sem=s2.at[q],
            recv_sem=r2.at[part],
            device_id=(q, taker),
            device_id_type=MESH,
        )

    def arrival(q):
        return pltpu.make_async_remote_copy(
            src_ref=mine,
            dst_ref=full.at[:, spot(q, chunk)],
            send_sem=s2.at[q],
            recv_sem=r2.at[q],
            device_id=(b, r),
            device_id_type=MESH,
        )

    for q in range(nb):
        own = q * nr + taker == me

        @pl.when(jnp.logical_not(own))
        def _():
            deliver(q).start()

        @pl.when(own)
        def _():
            full[:, spot(part, chunk)] = mine[...]

    for q in range(nb):

        @pl.when(r * nb + q != me)
        def _():
            arrival(q).wait_recv()

    for q in range(nb):

        @pl.when(q * nr + taker != me)
        def _():
            deliver(q).wait_send()

    o_ref[...] = full[...]


def turn_kernel(nb, nr, x_ref, add_ref, o_ref, land, mine, full, s1, r1, s2, r2):
    b, r = lax.axis_index("blk"), lax.axis_index("rows")
    me = b * nr + r
    chunk = land.shape[2]
    place = r * nb + b
    plane, part = place // nr, lax.rem(place, nr)
    barrier = pltpu.get_barrier_semaphore()
    for k in range(1, nb):
        pl.semaphore_signal(
            barrier, inc=1, device_id=(lax.rem(b + k, nb), r), device_id_type=MESH
        )

    def hello(p, carry):
        whose = b * nr + p
        side, line = lax.rem(whose, nb), whose // nb

        @pl.when(side * nr + line != me)
        def _():
            pl.semaphore_signal(barrier, inc=1, device_id=(side, line), device_id_type=MESH)

        return carry

    lax.fori_loop(0, nr, hello, 0)
    pl.semaphore_wait(barrier, nb - 1 + nr - (plane == b).astype(jnp.int32))

    def make(k):
        other = lax.rem(b + k, nb)
        return pltpu.make_async_remote_copy(
            src_ref=x_ref.at[:, spot(other, chunk)],
            dst_ref=land.at[b],
            send_sem=s1.at[k],
            recv_sem=r1.at[k],
            device_id=(other, r),
            device_id_type=MESH,
        )

    land[b] = x_ref[:, spot(b, chunk)]

    def add_up():
        mine[...] = add_parts(land) + add_ref[:, spot(b, chunk)]

    exchange(make, nb, add_up)

    def deliver(k):
        other = lax.rem(r + k, nr)
        return other, pltpu.make_async_remote_copy(
            src_ref=mine,
            dst_ref=full.at[:, spot(part, chunk)],
            send_sem=s2.at[k],
            recv_sem=r2.at[part],
            device_id=(plane, other),
            device_id_type=MESH,
        )

    def arrival(p):
        return pltpu.make_async_remote_copy(
            src_ref=mine,
            dst_ref=full.at[:, spot(p, chunk)],
            send_sem=s2.at[p],
            recv_sem=r2.at[p],
            device_id=(b, r),
            device_id_type=MESH,
        )

    def start(k, carry):
        deliver(k)[1].start()
        return carry

    def arrive(p, carry):
        whose = b * nr + p

        @pl.when(lax.rem(whose, nb) * nr + whose // nb != me)
        def _():
            arrival(p).wait_recv()

        return carry

    def left(k, carry):
        deliver(k)[1].wait_send()
        return carry

    @pl.when(plane != b)
    def _():
        deliver(0)[1].start()

    lax.fori_loop(1, nr, start, 0)

    @pl.when(plane == b)
    def _():
        full[:, spot(part, chunk)] = mine[...]

    lax.fori_loop(0, nr, arrive, 0)

    @pl.when(plane != b)
    def _():
        deliver(0)[1].wait_send()

    lax.fori_loop(1, nr, left, 0)
    o_ref[...] = full[...]


def swap_kernel(kind, nb, nr, x_ref, o_ref, land, s1, r1):
    b, r = lax.axis_index("blk"), lax.axis_index("rows")
    across = kind in ("pair", "images", "share")
    parts, own = (nb, b) if across else (nr, r)

    def device(k):
        other = lax.rem(own + k, parts)
        return (other, r) if across else (b, other)

    greet(device, parts)

    def make(k):
        source = x_ref.at[lax.rem(own + k, parts)] if kind == "move" else x_ref
        return pltpu.make_async_remote_copy(
            src_ref=source,
            dst_ref=land.at[own],
            send_sem=s1.at[k],
            recv_sem=r1.at[k],
            device_id=device(k),
            device_id_type=MESH,
        )

    land[own] = x_ref[own] if kind == "move" else x_ref[...]

    def finish():
        o_ref[...] = land[...] if kind in ("move", "share") else add_parts(land)

    exchange(make, parts, finish)


KINDS = ("plane", "slice", "turn", "pair", "images", "share", "total", "move")


def call(kind, body, nb, nr, shape, dtype, scratch, *operands):
    whole = pl.BlockSpec(memory_space=pltpu.VMEM)
    return pl.pallas_call(
        functools.partial(body, nb, nr),
        out_shape=jax.ShapeDtypeStruct(shape, dtype),
        in_specs=[whole] * len(operands),
        out_specs=whole,
        scratch_shapes=scratch,
        compiler_params=pltpu.CompilerParams(
            collective_id=KINDS.index(kind), has_side_effects=True
        ),
    )(*operands)


def plain(nb, nr):
    return nb * nr > 64 or nb != 2


dma = pltpu.SemaphoreType.DMA


def float_buffer(*shape):
    return pltpu.VMEM(shape, jnp.float32)


def plane_sum(nb, nr, x):
    if plain(nb, nr):
        return lax.psum(x, "rows")
    width = x.shape[1]
    scratch = [float_buffer(nr, PAD, width // nr), float_buffer(PAD, width)] + [dma((nr,))] * 4
    return call("plane", plane_kernel, nb, nr, x.shape, jnp.float32, scratch, x)


def slice_sum(nb, nr, x):
    size = x.shape[1] * nb // nr
    if plain(nb, nr):
        full = lax.all_gather(lax.psum(x, "rows"), "blk", axis=1, tiled=True)
        return lax.dynamic_slice_in_dim(full, lax.axis_index("rows") * size, size, 1)
    chunk = x.shape[1] // nr
    scratch = [
        float_buffer(nr, PAD, chunk),
        float_buffer(PAD, chunk),
        float_buffer(PAD, size),
        dma((nr,)),
        dma((nr,)),
        dma((nb,)),
        dma((nb,)),
    ]
    return call("slice", slice_kernel, nb, nr, (PAD, size), jnp.float32, scratch, x)


def turn_sum(nb, nr, x, add):
    width = x.shape[1] * nr // nb
    if plain(nb, nr):
        full = lax.all_gather(lax.psum(x, "blk") + add, "rows", axis=1, tiled=True)
        return lax.dynamic_slice_in_dim(full, lax.axis_index("blk") * width, width, 1)
    chunk = x.shape[1] // nb
    scratch = [
        float_buffer(nb, PAD, chunk),
        float_buffer(PAD, chunk),
        float_buffer(PAD, width),
        dma((nb,)),
        dma((nb,)),
        dma((nr,)),
        dma((nr,)),
    ]
    return call("turn", turn_kernel, nb, nr, (PAD, width), jnp.float32, scratch, x, add)


def swapped(kind, nb, nr, x):
    if plain(nb, nr):
        if kind == "total":
            return lax.psum(x, "rows")
        if kind == "move":
            return lax.all_to_all(x, "rows", split_axis=0, concat_axis=0, tiled=True)
        if kind == "share":
            return lax.all_gather(x, "blk", axis=0)
        return lax.psum(x, "blk")
    parts = nr if kind in ("total", "move") else nb
    land = x.shape if kind == "move" else (parts,) + x.shape
    shape = land if kind == "share" else x.shape
    scratch = [pltpu.VMEM(land, x.dtype), dma((parts,)), dma((parts,))]
    return call(kind, functools.partial(swap_kernel, kind), nb, nr, shape, x.dtype, scratch, x)


def three_parts(x):
    high = x.astype(jnp.bfloat16).astype(jnp.float32)
    rest = x - high
    mid = rest.astype(jnp.bfloat16).astype(jnp.float32)
    return high, mid, rest - mid


def exact_product(dims, vector, block):
    stacked = jnp.concatenate(three_parts(vector), axis=0).astype(jnp.bfloat16)
    total = None
    for part in reversed(three_parts(block)):
        product = lax.dot_general(
            stacked, part.astype(jnp.bfloat16), dims, preferred_element_type=jnp.float32
        )
        product = product[2 * PAD :] + product[PAD : 2 * PAD] + product[:PAD]
        total = product if total is None else total + product
    return total


def forward_kernel(u_ref, block_ref, o_ref):
    o_ref[...] = exact_product((((1,), (1,)), ((), ())), u_ref[...], block_ref[...])


def backward_kernel(u_ref, block_ref, o_ref):
    product = exact_product((((1,), (0,)), ((), ())), u_ref[...], block_ref[...])

    @pl.when(pl.program_id(0) == 0)
    def _():
        o_ref[...] = product

    @pl.when(pl.program_id(0) > 0)
    def _():
        o_ref[...] += product


STEP = 512


def factor_forward(block, vector):
    rows, cols = block.shape
    return pl.pallas_call(
        forward_kernel,
        grid=(rows // STEP,),
        in_specs=[
            pl.BlockSpec((PAD, cols), lambda i: (0, 0)),
            pl.BlockSpec((STEP, cols), lambda i: (i, 0)),
        ],
        out_specs=pl.BlockSpec((PAD, STEP), lambda i: (0, i)),
        out_shape=jax.ShapeDtypeStruct((PAD, rows), jnp.float32),
    )(vector, block)


def factor_backward(block, vector):
    rows, cols = block.shape
    return pl.pallas_call(
        backward_kernel,
        grid=(rows // STEP,),
        in_specs=[
            pl.BlockSpec((PAD, STEP), lambda i: (0, i)),
            pl.BlockSpec((STEP, cols), lambda i: (i, 0)),
        ],
        out_specs=pl.BlockSpec((PAD, cols), lambda i: (0, 0)),
        out_shape=jax.ShapeDtypeStruct((PAD, cols), jnp.float32),
    )(vector, block)


def square_norms(rows_x):
    return jnp.einsum("nd,nd->n", rows_x, rows_x, preferred_element_type=jnp.float32)


def factor_loop(forward, vector_ref, clean, block, p_ref):
    steps = block.shape[0] // STEP
    lines = lax.broadcasted_iota(jnp.int32, (PAD, STEP), 0)

    def visit(i, carry):
        piece = block[spot(i, STEP), :]
        if forward:
            p_ref[:, spot(i, STEP)] = exact_product(
                (((1,), (1,)), ((), ())), vector_ref[...], piece
            )
            return carry
        ours = vector_ref[:, spot(i, STEP)]
        if clean:
            ours = jnp.where(lines < CLASSES, ours, 0.0)
        p_ref[...] += exact_product((((1,), (0,)), ((), ())), ours, piece)
        return carry

    if not forward:
        p_ref[...] = jnp.zeros_like(p_ref)
    lax.fori_loop(0, steps, visit, 0)


def joint_kernel(kind, nb, nr, *refs):
    inputs = {"plane": 1, "slice": 1, "turn": 2, "pair": 3}[kind]
    block_ref, o_ref, p_ref, block, block_sem = refs[inputs : inputs + 5]
    rest = refs[inputs + 5 :]
    load = pltpu.make_async_copy(block_ref, block, block_sem)
    load.start()
    if kind == "plane":
        plane_kernel(nb, nr, refs[0], o_ref, *rest)
    elif kind == "slice":
        slice_kernel(nb, nr, refs[0], o_ref, *rest)
    elif kind == "turn":
        turn_kernel(nb, nr, refs[0], refs[1], o_ref, *rest)
    else:
        swap_kernel("pair", nb, nr, refs[0], o_ref, *rest)
        o_ref[...] = refs[1][...] + refs[2][...] * o_ref[...]
    load.wait()
    factor_loop(kind in ("slice", "pair"), o_ref, kind == "plane", block, p_ref)


def joint_sum(kind, nb, nr, block, *operands):
    rows, cols = block.shape
    x = operands[0]
    forward = kind in ("slice", "pair")
    if plain(nb, nr):
        if kind == "plane":
            out = plane_sum(nb, nr, x)
            lines = jnp.arange(PAD, dtype=jnp.int32)[:, None]
            return out, factor_backward(block, jnp.where(lines < CLASSES, out, 0.0))
        if kind == "turn":
            out = turn_sum(nb, nr, *operands)
            return out, factor_backward(block, out)
        if kind == "slice":
            out = slice_sum(nb, nr, x)
        else:
            out = operands[1] + operands[2] * swapped("pair", nb, nr, x)
        return out, factor_forward(block, out)
    size, wide = (cols, rows) if forward else (rows, cols)
    if kind == "plane":
        chunk = rows // nr
        scratch = [float_buffer(nr, PAD, chunk), float_buffer(PAD, rows)] + [dma((nr,))] * 4
    elif kind == "pair":
        scratch = [float_buffer(nb, PAD, cols), dma((nb,)), dma((nb,))]
    else:
        first, then = (nr, nb) if kind == "slice" else (nb, nr)
        chunk = cols // nb
        scratch = [float_buffer(first, PAD, chunk), float_buffer(PAD, chunk), float_buffer(PAD, size)]
        scratch += [dma((first,))] * 2 + [dma((then,))] * 2
    whole = pl.BlockSpec(memory_space=pltpu.VMEM)
    return pl.pallas_call(
        functools.partial(joint_kernel, kind, nb, nr),
        out_shape=(
            jax.ShapeDtypeStruct((PAD, size), jnp.float32),
            jax.ShapeDtypeStruct((PAD, wide), jnp.float32),
        ),
        in_specs=[whole] * len(operands) + [pl.BlockSpec(memory_space=pl.ANY)],
        out_specs=(whole, whole),
        scratch_shapes=[float_buffer(rows, cols), dma] + scratch,
        compiler_params=pltpu.CompilerParams(
            collective_id=len(KINDS) + ("plane", "slice", "turn", "pair").index(kind),
            has_side_effects=True,
            vmem_limit_bytes=32 * 1024 * 1024,
        ),
    )(*operands, block)


def to_low(values):
    return lax.reduce_precision(values, 8, 7).astype(jnp.bfloat16)


def with_scalars(vector, scalars):
    return vector + jnp.pad(scalars[None, :], ((PAD - 1, 0), (0, vector.shape[1] - PAD)))


def on_device(nb, nr, features, labels, destination, centres, tri_inverse, aux_inverse):
    own_rows, width = features.shape
    capacity = max(2, 2 * own_rows // nr)
    scale = 2.0 / width
    count_all = float(own_rows * nb * nr)
    b = lax.axis_index("blk")
    class_rows = jnp.arange(PAD, dtype=jnp.int32)[:, None]
    real = class_rows < CLASSES

    tags = jnp.pad(labels.astype(jnp.bfloat16), (0, -own_rows % (16 * width)))
    tags = tags.reshape(-1, width)
    shared = swapped("share", nb, nr, jnp.concatenate([features, tags], axis=0))
    rows_x = shared[:, :own_rows].reshape(nb * own_rows, width)
    tags = shared[:, own_rows:].reshape(nb, -1)[:, :own_rows].reshape(nb * own_rows)
    centre_norm = square_norms(centres)
    rows_norm = square_norms(rows_x)
    inner = lax.dot_general(
        rows_x, centres, (((1,), (1,)), ((), ())), preferred_element_type=jnp.float32
    )
    kmat = jnp.exp(-(rows_norm[:, None] + centre_norm[None, :] - 2.0 * inner) * scale).astype(
        jnp.bfloat16
    )
    hits = tags.astype(jnp.float32)[None, :] == class_rows.astype(jnp.float32)
    targets = jnp.where(real, jnp.where(hits, 1.0, -1.0), 0.0).astype(jnp.bfloat16)

    def clean(vector):
        return jnp.where(real, vector, 0.0)

    def onto_rows(low):
        return lax.dot_general(
            low, kmat, (((1,), (1,)), ((), ())), preferred_element_type=jnp.float32
        )

    def images(second):
        high = to_low(second)
        rest = second - high.astype(jnp.float32)
        mid = to_low(rest)
        low = to_low(rest - mid.astype(jnp.float32))
        three = onto_rows(jnp.concatenate([high, mid, low], axis=0))
        both = jnp.concatenate([three[:PAD], three[PAD : 2 * PAD] + three[2 * PAD :]], axis=0)
        both = swapped("images", nb, nr, both)
        image = to_low(both[:PAD])
        exact = both[:PAD] + both[PAD:]
        curve = jnp.sum(image.astype(jnp.float32) * exact, axis=1) / count_all
        return image, curve

    def ratio(above, below):
        return jnp.where(real, (above / below)[:, None], 0.0)

    def normal(vector):
        return jnp.sum(vector * vector, axis=1)

    start = jnp.dot(targets, kmat, preferred_element_type=jnp.float32) / count_all
    start = joint_sum("plane", nb, nr, tri_inverse, start)[1]
    start = joint_sum("turn", nb, nr, aux_inverse, start, jnp.zeros_like(start))[1]
    zeros = jnp.zeros_like(start)
    rhs, start = joint_sum("pair", nb, nr, aux_inverse, start, zeros, zeros + 1.0)
    first, start = joint_sum("slice", nb, nr, tri_inverse, start)
    joined = plane_sum(nb, nr, with_scalars(start, normal(rhs)))
    norm_first = joined[PAD - 1, :PAD]
    second = clean(joined)
    image, curve = images(second)
    curve = curve + ridge_weight * normal(first)
    gram = jnp.dot(image, kmat, preferred_element_type=jnp.float32) / count_all
    joined, turned = joint_sum("plane", nb, nr, tri_inverse, with_scalars(gram, curve))
    step_first = ratio(norm_first, joined[PAD - 1, :PAD])
    turned = joint_sum("turn", nb, nr, aux_inverse, turned, ridge_weight * first)[1]
    residual, start = joint_sum("pair", nb, nr, aux_inverse, turned, rhs, zeros - step_first)
    first_next, start = joint_sum("slice", nb, nr, tri_inverse, start)
    joined = plane_sum(nb, nr, with_scalars(start, normal(residual)))
    norm_next = joined[PAD - 1, :PAD]
    turn_weight = ratio(norm_next, norm_first)
    first_next = first_next + turn_weight * first
    second_next = clean(joined) + turn_weight * second
    image, curve = images(second_next)
    curve = curve + ridge_weight * normal(first_next)
    curve = swapped("total", nb, nr, jnp.pad(curve[:, None], ((0, 0), (0, 127))))[:, 0]
    step_next = ratio(norm_next, curve)
    coefficients = step_first * second + step_next * second_next
    scores = swapped("pair", nb, nr, onto_rows(to_low(coefficients)))
    scores = lax.dynamic_slice_in_dim(scores, b * own_rows, own_rows, 1)

    target = destination[:, 0]
    row_ids = jnp.arange(own_rows, dtype=jnp.int32)
    same = (target[:, None] == target[None, :]) & (row_ids[None, :] < row_ids[:, None])
    before = jnp.sum(same.astype(jnp.int32), axis=1)
    slots = nr * capacity
    spread = (
        (target * capacity + before)[:, None] == jnp.arange(slots, dtype=jnp.int32)[None, :]
    ).astype(jnp.float32)
    placed = jnp.dot(scores, spread, precision=highest, preferred_element_type=jnp.float32)
    placed = placed.reshape(PAD, nr, capacity).transpose(1, 0, 2)
    lanes = -capacity % 128
    moved = swapped("move", nb, nr, jnp.pad(placed, ((0, 0), (0, 0), (0, lanes))))
    moved = moved[:, :CLASSES, :capacity]
    return moved.transpose(1, 0, 2).reshape(CLASSES, slots)


def solution(mesh):
    return jax.shard_map(
        functools.partial(on_device, mesh.shape["blk"], mesh.shape["rows"]),
        mesh=mesh,
        in_specs=(
            P(("blk", "rows"), None),
            P(("blk", "rows")),
            P(("blk", "rows"), None),
            P("blk", None),
            P("blk", "rows"),
            P("blk", "rows"),
        ),
        out_specs=P(None, ("blk", "rows")),
        check_vma=False,
    )
```

```python
import functools

import jax
import jax.numpy as jnp
from jax import lax
from jax.experimental import pallas as pl
from jax.experimental.pallas import tpu as pltpu
from jax.sharding import PartitionSpec as P

CLASSES = 7
PAD = 8
MESH = pl.DeviceIdType.MESH
ridge_weight = 0.1
highest = lax.Precision.HIGHEST


def greet(peers, count):
    barrier = pltpu.get_barrier_semaphore()

    def hello(k, carry):
        pl.semaphore_signal(barrier, inc=1, device_id=peers(k), device_id_type=MESH)
        return carry

    lax.fori_loop(1, count, hello, 0)
    pl.semaphore_wait(barrier, count - 1)


def exchange(make, count, then, meanwhile=None):
    def send(k, carry):
        make(k).start()
        return carry

    def arrive(k, carry):
        make(k).wait_recv()
        return carry

    def left(k, carry):
        make(k).wait_send()
        return carry

    lax.fori_loop(1, count, send, 0)
    if meanwhile is not None:
        meanwhile()
    lax.fori_loop(1, count, arrive, 0)
    if then is not None:
        then()
    lax.fori_loop(1, count, left, 0)


def spot(index, chunk):
    return pl.ds(pl.multiple_of(index * chunk, chunk), chunk)


def add_parts(land):
    total = land[0]
    for index in range(1, land.shape[0]):
        total = total + land[index]
    return total


def spread_rows(nr, chunk, x_ref, land, s1, r1):
    b, r = lax.axis_index("blk"), lax.axis_index("rows")

    def make(k):
        other = lax.rem(r + k, nr)
        return pltpu.make_async_remote_copy(
            src_ref=x_ref.at[:, spot(other, chunk)],
            dst_ref=land.at[r],
            send_sem=s1.at[k],
            recv_sem=r1.at[k],
            device_id=(b, other),
            device_id_type=MESH,
        )

    land[r] = x_ref[:, spot(r, chunk)]
    return make


def plane_kernel(nb, nr, x_ref, o_ref, land, full, s1, r1, s2, r2, meanwhile=None):
    b, r = lax.axis_index("blk"), lax.axis_index("rows")
    chunk = land.shape[2]
    greet(lambda k: (b, lax.rem(r + k, nr)), nr)
    make = spread_rows(nr, chunk, x_ref, land, s1, r1)

    def add_up():
        full[:, spot(r, chunk)] = add_parts(land)

    exchange(make, nr, add_up)

    def gather(k):
        return pltpu.make_async_remote_copy(
            src_ref=full.at[:, spot(r, chunk)],
            dst_ref=full.at[:, spot(r, chunk)],
            send_sem=s2.at[k],
            recv_sem=r2.at[k],
            device_id=(b, lax.rem(r + k, nr)),
            device_id_type=MESH,
        )

    exchange(gather, nr, None, meanwhile)
    o_ref[...] = full[...]


def slice_kernel(nb, nr, x_ref, o_ref, land, mine, full, s1, r1, s2, r2, meanwhile):
    b, r = lax.axis_index("blk"), lax.axis_index("rows")
    me = b * nr + r
    chunk = land.shape[2]
    barrier = pltpu.get_barrier_semaphore()

    def hello(k, carry):
        pl.semaphore_signal(
            barrier, inc=1, device_id=(b, lax.rem(r + k, nr)), device_id_type=MESH
        )
        return carry

    lax.fori_loop(1, nr, hello, 0)
    for q in range(nb):
        source = r * nb + q

        @pl.when(source // nr != b)
        def _():
            pl.semaphore_signal(
                barrier,
                inc=1,
                device_id=(source // nr, lax.rem(source, nr)),
                device_id_type=MESH,
            )

    pl.semaphore_wait(barrier, nr - 1 + nb - 1)
    make = spread_rows(nr, chunk, x_ref, land, s1, r1)

    def add_up():
        mine[...] = add_parts(land)

    exchange(make, nr, add_up)
    taker, part = me // nb, lax.rem(me, nb)

    def deliver(q):
        return pltpu.make_async_remote_copy(
            src_ref=mine,
            dst_ref=full.at[:, spot(part, chunk)],
            send_sem=s2.at[q],
            recv_sem=r2.at[part],
            device_id=(q, taker),
            device_id_type=MESH,
        )

    def arrival(q):
        return pltpu.make_async_remote_copy(
            src_ref=mine,
            dst_ref=full.at[:, spot(q, chunk)],
            send_sem=s2.at[q],
            recv_sem=r2.at[q],
            device_id=(b, r),
            device_id_type=MESH,
        )

    for q in range(nb):
        own = q * nr + taker == me

        @pl.when(jnp.logical_not(own))
        def _():
            deliver(q).start()

        @pl.when(own)
        def _():
            full[:, spot(part, chunk)] = mine[...]

    meanwhile()
    for q in range(nb):

        @pl.when(r * nb + q != me)
        def _():
            arrival(q).wait_recv()

    for q in range(nb):

        @pl.when(q * nr + taker != me)
        def _():
            deliver(q).wait_send()

    o_ref[...] = full[...]


def turn_kernel(nb, nr, x_ref, add_ref, o_ref, land, mine, full, s1, r1, s2, r2, meanwhile):
    b, r = lax.axis_index("blk"), lax.axis_index("rows")
    me = b * nr + r
    chunk = land.shape[2]
    place = r * nb + b
    plane, part = place // nr, lax.rem(place, nr)
    barrier = pltpu.get_barrier_semaphore()
    for k in range(1, nb):
        pl.semaphore_signal(
            barrier, inc=1, device_id=(lax.rem(b + k, nb), r), device_id_type=MESH
        )

    def hello(p, carry):
        whose = b * nr + p
        side, line = lax.rem(whose, nb), whose // nb

        @pl.when(side * nr + line != me)
        def _():
            pl.semaphore_signal(barrier, inc=1, device_id=(side, line), device_id_type=MESH)

        return carry

    lax.fori_loop(0, nr, hello, 0)
    pl.semaphore_wait(barrier, nb - 1 + nr - (plane == b).astype(jnp.int32))

    def make(k):
        other = lax.rem(b + k, nb)
        return pltpu.make_async_remote_copy(
            src_ref=x_ref.at[:, spot(other, chunk)],
            dst_ref=land.at[b],
            send_sem=s1.at[k],
            recv_sem=r1.at[k],
            device_id=(other, r),
            device_id_type=MESH,
        )

    land[b] = x_ref[:, spot(b, chunk)]

    def add_up():
        mine[...] = add_parts(land) + add_ref[:, spot(b, chunk)]

    exchange(make, nb, add_up)

    def deliver(k):
        other = lax.rem(r + k, nr)
        return other, pltpu.make_async_remote_copy(
            src_ref=mine,
            dst_ref=full.at[:, spot(part, chunk)],
            send_sem=s2.at[k],
            recv_sem=r2.at[part],
            device_id=(plane, other),
            device_id_type=MESH,
        )

    def arrival(p):
        return pltpu.make_async_remote_copy(
            src_ref=mine,
            dst_ref=full.at[:, spot(p, chunk)],
            send_sem=s2.at[p],
            recv_sem=r2.at[p],
            device_id=(b, r),
            device_id_type=MESH,
        )

    def start(k, carry):
        deliver(k)[1].start()
        return carry

    def arrive(p, carry):
        whose = b * nr + p

        @pl.when(lax.rem(whose, nb) * nr + whose // nb != me)
        def _():
            arrival(p).wait_recv()

        return carry

    def left(k, carry):
        deliver(k)[1].wait_send()
        return carry

    @pl.when(plane != b)
    def _():
        deliver(0)[1].start()

    lax.fori_loop(1, nr, start, 0)

    @pl.when(plane == b)
    def _():
        full[:, spot(part, chunk)] = mine[...]

    meanwhile()
    lax.fori_loop(0, nr, arrive, 0)

    @pl.when(plane != b)
    def _():
        deliver(0)[1].wait_send()

    lax.fori_loop(1, nr, left, 0)
    o_ref[...] = full[...]


def swap_kernel(kind, nb, nr, x_ref, o_ref, land, s1, r1, meanwhile=None):
    b, r = lax.axis_index("blk"), lax.axis_index("rows")
    across = kind in ("pair", "images", "share")
    parts, own = (nb, b) if across else (nr, r)

    def device(k):
        other = lax.rem(own + k, parts)
        return (other, r) if across else (b, other)

    greet(device, parts)

    def make(k):
        source = x_ref.at[lax.rem(own + k, parts)] if kind == "move" else x_ref
        return pltpu.make_async_remote_copy(
            src_ref=source,
            dst_ref=land.at[own],
            send_sem=s1.at[k],
            recv_sem=r1.at[k],
            device_id=device(k),
            device_id_type=MESH,
        )

    land[own] = x_ref[own] if kind == "move" else x_ref[...]

    def finish():
        o_ref[...] = land[...] if kind in ("move", "share") else add_parts(land)

    exchange(make, parts, finish, meanwhile)


KINDS = ("plane", "slice", "turn", "pair", "images", "share", "total", "move")


def call(kind, body, nb, nr, shape, dtype, scratch, *operands):
    whole = pl.BlockSpec(memory_space=pltpu.VMEM)
    return pl.pallas_call(
        functools.partial(body, nb, nr),
        out_shape=jax.ShapeDtypeStruct(shape, dtype),
        in_specs=[whole] * len(operands),
        out_specs=whole,
        scratch_shapes=scratch,
        compiler_params=pltpu.CompilerParams(
            collective_id=KINDS.index(kind), has_side_effects=True
        ),
    )(*operands)


def plain(nb, nr):
    return nb * nr > 64 or nb != 2


dma = pltpu.SemaphoreType.DMA


def float_buffer(*shape):
    return pltpu.VMEM(shape, jnp.float32)


def plane_sum(nb, nr, x):
    if plain(nb, nr):
        return lax.psum(x, "rows")
    width = x.shape[1]
    scratch = [float_buffer(nr, PAD, width // nr), float_buffer(PAD, width)] + [dma((nr,))] * 4
    return call("plane", plane_kernel, nb, nr, x.shape, jnp.float32, scratch, x)


def slice_sum(nb, nr, x):
    size = x.shape[1] * nb // nr
    if plain(nb, nr):
        full = lax.all_gather(lax.psum(x, "rows"), "blk", axis=1, tiled=True)
        return lax.dynamic_slice_in_dim(full, lax.axis_index("rows") * size, size, 1)
    chunk = x.shape[1] // nr
    scratch = [
        float_buffer(nr, PAD, chunk),
        float_buffer(PAD, chunk),
        float_buffer(PAD, size),
        dma((nr,)),
        dma((nr,)),
        dma((nb,)),
        dma((nb,)),
    ]
    return call("slice", slice_kernel, nb, nr, (PAD, size), jnp.float32, scratch, x)


def turn_sum(nb, nr, x, add):
    width = x.shape[1] * nr // nb
    if plain(nb, nr):
        full = lax.all_gather(lax.psum(x, "blk") + add, "rows", axis=1, tiled=True)
        return lax.dynamic_slice_in_dim(full, lax.axis_index("blk") * width, width, 1)
    chunk = x.shape[1] // nb
    scratch = [
        float_buffer(nb, PAD, chunk),
        float_buffer(PAD, chunk),
        float_buffer(PAD, width),
        dma((nb,)),
        dma((nb,)),
        dma((nr,)),
        dma((nr,)),
    ]
    return call("turn", turn_kernel, nb, nr, (PAD, width), jnp.float32, scratch, x, add)


def swapped(kind, nb, nr, x):
    if plain(nb, nr):
        if kind == "total":
            return lax.psum(x, "rows")
        if kind == "move":
            return lax.all_to_all(x, "rows", split_axis=0, concat_axis=0, tiled=True)
        if kind == "share":
            return lax.all_gather(x, "blk", axis=0)
        return lax.psum(x, "blk")
    parts = nr if kind in ("total", "move") else nb
    land = x.shape if kind == "move" else (parts,) + x.shape
    shape = land if kind == "share" else x.shape
    scratch = [pltpu.VMEM(land, x.dtype), dma((parts,)), dma((parts,))]
    return call(kind, functools.partial(swap_kernel, kind), nb, nr, shape, x.dtype, scratch, x)


def three_parts(x):
    high = x.astype(jnp.bfloat16).astype(jnp.float32)
    rest = x - high
    mid = rest.astype(jnp.bfloat16).astype(jnp.float32)
    return high, mid, rest - mid


def exact_product(dims, vector, block):
    stacked = jnp.concatenate(three_parts(vector), axis=0).astype(jnp.bfloat16)
    total = None
    for part in reversed(block):
        product = lax.dot_general(
            stacked, part.astype(jnp.bfloat16), dims, preferred_element_type=jnp.float32
        )
        product = product[2 * PAD :] + product[PAD : 2 * PAD] + product[:PAD]
        total = product if total is None else total + product
    return total


def forward_kernel(u_ref, block_ref, o_ref):
    o_ref[...] = exact_product((((1,), (1,)), ((), ())), u_ref[...], three_parts(block_ref[...]))


def backward_kernel(u_ref, block_ref, o_ref):
    product = exact_product((((1,), (0,)), ((), ())), u_ref[...], three_parts(block_ref[...]))

    @pl.when(pl.program_id(0) == 0)
    def _():
        o_ref[...] = product

    @pl.when(pl.program_id(0) > 0)
    def _():
        o_ref[...] += product


STEP = 512


def factor_forward(block, vector):
    rows, cols = block.shape
    return pl.pallas_call(
        forward_kernel,
        grid=(rows // STEP,),
        in_specs=[
            pl.BlockSpec((PAD, cols), lambda i: (0, 0)),
            pl.BlockSpec((STEP, cols), lambda i: (i, 0)),
        ],
        out_specs=pl.BlockSpec((PAD, STEP), lambda i: (0, i)),
        out_shape=jax.ShapeDtypeStruct((PAD, rows), jnp.float32),
    )(vector, block)


def factor_backward(block, vector):
    rows, cols = block.shape
    return pl.pallas_call(
        backward_kernel,
        grid=(rows // STEP,),
        in_specs=[
            pl.BlockSpec((PAD, STEP), lambda i: (0, i)),
            pl.BlockSpec((STEP, cols), lambda i: (i, 0)),
        ],
        out_specs=pl.BlockSpec((PAD, cols), lambda i: (0, 0)),
        out_shape=jax.ShapeDtypeStruct((PAD, cols), jnp.float32),
    )(vector, block)


def square_norms(rows_x):
    return jnp.einsum("nd,nd->n", rows_x, rows_x, preferred_element_type=jnp.float32)


def factor_loop(forward, vector_ref, clean, block, p_ref):
    steps = block.shape[1] // STEP
    lines = lax.broadcasted_iota(jnp.int32, (PAD, STEP), 0)

    def visit(i, carry):
        piece = [block[index, spot(i, STEP), :] for index in range(3)]
        if forward:
            p_ref[:, spot(i, STEP)] = exact_product(
                (((1,), (1,)), ((), ())), vector_ref[...], piece
            )
            return carry
        ours = vector_ref[:, spot(i, STEP)]
        if clean:
            ours = jnp.where(lines < CLASSES, ours, 0.0)
        p_ref[...] += exact_product((((1,), (0,)), ((), ())), ours, piece)
        return carry

    if not forward:
        p_ref[...] = jnp.zeros_like(p_ref)
    lax.fori_loop(0, steps, visit, 0)


def joint_kernel(kind, nb, nr, *refs):
    inputs = {"plane": 1, "slice": 1, "turn": 2, "pair": 3}[kind]
    block_ref, o_ref, p_ref, block, split, block_sem = refs[inputs : inputs + 6]
    rest = refs[inputs + 6 :]
    load = pltpu.make_async_copy(block_ref, block, block_sem)
    load.start()

    def meanwhile():
        load.wait()

        def visit(i, carry):
            piece = spot(i, STEP)
            for index, part in enumerate(three_parts(block[piece, :])):
                split[index, piece, :] = part.astype(jnp.bfloat16)
            return carry

        lax.fori_loop(0, block.shape[0] // STEP, visit, 0)

    if kind == "plane":
        plane_kernel(nb, nr, refs[0], o_ref, *rest, meanwhile)
    elif kind == "slice":
        slice_kernel(nb, nr, refs[0], o_ref, *rest, meanwhile)
    elif kind == "turn":
        turn_kernel(nb, nr, refs[0], refs[1], o_ref, *rest, meanwhile)
    else:
        swap_kernel("pair", nb, nr, refs[0], o_ref, *rest, meanwhile)
        o_ref[...] = refs[1][...] + refs[2][...] * o_ref[...]
    factor_loop(kind in ("slice", "pair"), o_ref, kind == "plane", split, p_ref)


def joint_sum(kind, nb, nr, block, *operands):
    rows, cols = block.shape
    x = operands[0]
    forward = kind in ("slice", "pair")
    if plain(nb, nr):
        if kind == "plane":
            out = plane_sum(nb, nr, x)
            lines = jnp.arange(PAD, dtype=jnp.int32)[:, None]
            return out, factor_backward(block, jnp.where(lines < CLASSES, out, 0.0))
        if kind == "turn":
            out = turn_sum(nb, nr, *operands)
            return out, factor_backward(block, out)
        if kind == "slice":
            out = slice_sum(nb, nr, x)
        else:
            out = operands[1] + operands[2] * swapped("pair", nb, nr, x)
        return out, factor_forward(block, out)
    size, wide = (cols, rows) if forward else (rows, cols)
    if kind == "plane":
        chunk = rows // nr
        scratch = [float_buffer(nr, PAD, chunk), float_buffer(PAD, rows)] + [dma((nr,))] * 4
    elif kind == "pair":
        scratch = [float_buffer(nb, PAD, cols), dma((nb,)), dma((nb,))]
    else:
        first, then = (nr, nb) if kind == "slice" else (nb, nr)
        chunk = cols // nb
        scratch = [float_buffer(first, PAD, chunk), float_buffer(PAD, chunk), float_buffer(PAD, size)]
        scratch += [dma((first,))] * 2 + [dma((then,))] * 2
    whole = pl.BlockSpec(memory_space=pltpu.VMEM)
    return pl.pallas_call(
        functools.partial(joint_kernel, kind, nb, nr),
        out_shape=(
            jax.ShapeDtypeStruct((PAD, size), jnp.float32),
            jax.ShapeDtypeStruct((PAD, wide), jnp.float32),
        ),
        in_specs=[whole] * len(operands) + [pl.BlockSpec(memory_space=pltpu.MemorySpace.HBM)],
        out_specs=(whole, whole),
        scratch_shapes=[float_buffer(rows, cols), pltpu.VMEM((3, rows, cols), jnp.bfloat16), dma]
        + scratch,
        compiler_params=pltpu.CompilerParams(
            collective_id=len(KINDS) + ("plane", "slice", "turn", "pair").index(kind),
            has_side_effects=True,
            vmem_limit_bytes=32 * 1024 * 1024,
        ),
    )(*operands, block)


def to_low(values):
    return lax.reduce_precision(values, 8, 7).astype(jnp.bfloat16)


def with_scalars(vector, scalars):
    return vector + jnp.pad(scalars[None, :], ((PAD - 1, 0), (0, vector.shape[1] - PAD)))


def on_device(nb, nr, features, labels, destination, centres, tri_inverse, aux_inverse):
    own_rows, width = features.shape
    capacity = max(2, 2 * own_rows // nr)
    scale = 2.0 / width
    count_all = float(own_rows * nb * nr)
    b = lax.axis_index("blk")
    class_rows = jnp.arange(PAD, dtype=jnp.int32)[:, None]
    real = class_rows < CLASSES

    tags = jnp.pad(labels.astype(jnp.bfloat16), (0, -own_rows % (16 * width)))
    tags = tags.reshape(-1, width)
    shared = swapped("share", nb, nr, jnp.concatenate([features, tags], axis=0))
    rows_x = shared[:, :own_rows].reshape(nb * own_rows, width)
    tags = shared[:, own_rows:].reshape(nb, -1)[:, :own_rows].reshape(nb * own_rows)
    centre_norm = square_norms(centres)
    rows_norm = square_norms(rows_x)
    inner = lax.dot_general(
        rows_x, centres, (((1,), (1,)), ((), ())), preferred_element_type=jnp.float32
    )
    kmat = jnp.exp(-(rows_norm[:, None] + centre_norm[None, :] - 2.0 * inner) * scale).astype(
        jnp.bfloat16
    )
    hits = tags.astype(jnp.float32)[None, :] == class_rows.astype(jnp.float32)
    targets = jnp.where(real, jnp.where(hits, 1.0, -1.0), 0.0).astype(jnp.bfloat16)

    def clean(vector):
        return jnp.where(real, vector, 0.0)

    def onto_rows(low):
        return lax.dot_general(
            low, kmat, (((1,), (1,)), ((), ())), preferred_element_type=jnp.float32
        )

    def images(second):
        high = to_low(second)
        rest = second - high.astype(jnp.float32)
        mid = to_low(rest)
        low = to_low(rest - mid.astype(jnp.float32))
        three = onto_rows(jnp.concatenate([high, mid, low], axis=0))
        both = jnp.concatenate([three[:PAD], three[PAD : 2 * PAD] + three[2 * PAD :]], axis=0)
        both = swapped("images", nb, nr, both)
        image = to_low(both[:PAD])
        exact = both[:PAD] + both[PAD:]
        curve = jnp.sum(image.astype(jnp.float32) * exact, axis=1) / count_all
        return image, curve

    def ratio(above, below):
        return jnp.where(real, (above / below)[:, None], 0.0)

    def normal(vector):
        return jnp.sum(vector * vector, axis=1)

    start = jnp.dot(targets, kmat, preferred_element_type=jnp.float32) / count_all
    start = joint_sum("plane", nb, nr, tri_inverse, start)[1]
    start = joint_sum("turn", nb, nr, aux_inverse, start, jnp.zeros_like(start))[1]
    zeros = jnp.zeros_like(start)
    rhs, start = joint_sum("pair", nb, nr, aux_inverse, start, zeros, zeros + 1.0)
    first, start = joint_sum("slice", nb, nr, tri_inverse, start)
    joined = plane_sum(nb, nr, with_scalars(start, normal(rhs)))
    norm_first = joined[PAD - 1, :PAD]
    second = clean(joined)
    image, curve = images(second)
    curve = curve + ridge_weight * normal(first)
    gram = jnp.dot(image, kmat, preferred_element_type=jnp.float32) / count_all
    joined, turned = joint_sum("plane", nb, nr, tri_inverse, with_scalars(gram, curve))
    step_first = ratio(norm_first, joined[PAD - 1, :PAD])
    turned = joint_sum("turn", nb, nr, aux_inverse, turned, ridge_weight * first)[1]
    residual, start = joint_sum("pair", nb, nr, aux_inverse, turned, rhs, zeros - step_first)
    first_next, start = joint_sum("slice", nb, nr, tri_inverse, start)
    joined = plane_sum(nb, nr, with_scalars(start, normal(residual)))
    norm_next = joined[PAD - 1, :PAD]
    turn_weight = ratio(norm_next, norm_first)
    first_next = first_next + turn_weight * first
    second_next = clean(joined) + turn_weight * second
    image, curve = images(second_next)
    curve = curve + ridge_weight * normal(first_next)
    curve = swapped("total", nb, nr, jnp.pad(curve[:, None], ((0, 0), (0, 127))))[:, 0]
    step_next = ratio(norm_next, curve)
    coefficients = step_first * second + step_next * second_next
    scores = swapped("pair", nb, nr, onto_rows(to_low(coefficients)))
    scores = lax.dynamic_slice_in_dim(scores, b * own_rows, own_rows, 1)

    target = destination[:, 0]
    row_ids = jnp.arange(own_rows, dtype=jnp.int32)
    same = (target[:, None] == target[None, :]) & (row_ids[None, :] < row_ids[:, None])
    before = jnp.sum(same.astype(jnp.int32), axis=1)
    slots = nr * capacity
    spread = (
        (target * capacity + before)[:, None] == jnp.arange(slots, dtype=jnp.int32)[None, :]
    ).astype(jnp.float32)
    placed = jnp.dot(scores, spread, precision=highest, preferred_element_type=jnp.float32)
    placed = placed.reshape(PAD, nr, capacity).transpose(1, 0, 2)
    lanes = -capacity % 128
    moved = swapped("move", nb, nr, jnp.pad(placed, ((0, 0), (0, 0), (0, lanes))))
    moved = moved[:, :CLASSES, :capacity]
    return moved.transpose(1, 0, 2).reshape(CLASSES, slots)


def solution(mesh):
    return jax.shard_map(
        functools.partial(on_device, mesh.shape["blk"], mesh.shape["rows"]),
        mesh=mesh,
        in_specs=(
            P(("blk", "rows"), None),
            P(("blk", "rows")),
            P(("blk", "rows"), None),
            P("blk", None),
            P("blk", "rows"),
            P("blk", "rows"),
        ),
        out_specs=P(None, ("blk", "rows")),
        check_vma=False,
    )
```
